256 devices in a mesh: row: 8 (over x, core), col: 32 (over y, z).
Axes of the slice: x: 4, y: 4, z: 8, core: 2. Of those that a mesh axis runs over, the one named last changes fastest.
Arguments:
- kernel: float32 [16384, 16384], P('row', 'col'), as said below
Outputs:
- factored: float32 [16384, 16384], P('row', 'col')
Inputs may be any that keep to these rules, and one draw needn't show every extreme that they name: `kernel`: in logical order the matrix is symmetric and positive definite, with smallest eigenvalue 0.3 or more.
All inputs are finite; a program needn't handle non-finite values.
Results may differ from the reference program's by a relative error of at most 0.0003.
Values sent between devices are 32-bit elements; how exact they have to be, the bound alone decides.
A program may use at most 64 MiB of HBM per device.

```python
import math
import jax
import jax.numpy as jnp
from jax import lax

M = 16384
NB = 256
GRID_R = 8
GRID_C = 32
N_ROW = 8
N_COL = 32


def draw_kernel(key, part):
    key_off = jax.random.fold_in(key, 11)
    key_diag = jax.random.fold_in(key, 12)
    raw = jnp.clip(jax.random.normal(key_off, (M, M), jnp.float32), -4.0, 4.0)
    diag = jnp.exp(jax.random.uniform(key_diag, (M,), jnp.float32, math.log(2.5), math.log(5.0)))
    symmetric = (raw + raw.T) * (0.70710678 / math.sqrt(M))
    index = jnp.arange(M, dtype=jnp.int32)
    full = jnp.where(index[:, None] == index[None, :], diag[:, None], symmetric)
    distance = (index[:, None] - index[None, :]).astype(jnp.float32) * (1.0 / 64.0)
    full = full + 2.0 * jnp.exp(-0.5 * distance * distance)
    full = full.reshape(M // (NB * GRID_R), GRID_R, NB, M).transpose(1, 0, 2, 3).reshape(M, M)
    full = full.reshape(M, M // (NB * GRID_C), GRID_C, NB).transpose(0, 2, 1, 3).reshape(M, M)
    return full


def setup_inputs(seed: int = 0) -> dict:
    splits = jax.random.split(jax.random.key(seed), 2)
    kernel = draw_kernel(jax.random.fold_in(splits[1], 71), 0)
    return dict(kernel=kernel)


def product(first_op, second_op):
    return lax.dot_general(first_op.astype(jnp.float32), second_op.astype(jnp.float32), (((1,), (1,)), ((), ())), precision=lax.Precision.HIGHEST, preferred_element_type=jnp.float32)

def solve_panel(factor_low, row_data):
    return jax.scipy.linalg.solve_triangular(factor_low, row_data.T, lower=True).T

def reference(kernel):
    index = jnp.arange(M, dtype=jnp.int32)
    row_order = index.reshape(M // (NB * N_ROW), N_ROW, NB).transpose(1, 0, 2).reshape(M)
    col_order = index.reshape(M // (NB * N_COL), N_COL, NB).transpose(1, 0, 2).reshape(M)
    row_bid = row_order // NB
    col_bid = col_order // NB
    rows_dev = M // N_ROW
    cols_dev = M // N_COL
    first_raw = kernel[:, 0:NB]
    first_low = jnp.linalg.cholesky(first_raw[0:NB])
    first_solve = solve_panel(first_low, first_raw)
    first_used = jnp.where(row_bid[:, None] > 0, first_solve, 0.0)
    second_raw = kernel[:, cols_dev:cols_dev + NB] - product(first_used, first_used[rows_dev:rows_dev + NB])
    second_low = jnp.linalg.cholesky(second_raw[rows_dev:rows_dev + NB])
    second_solve = solve_panel(second_low, second_raw)
    second_used = jnp.where(row_bid[:, None] > 1, second_solve, 0.0)
    row_pos = col_order // NB % N_ROW * rows_dev + col_order // (NB * N_ROW) * NB + col_order % NB
    first_cols = first_used[row_pos]
    second_cols = second_used[row_pos]
    tiled_one = jnp.tile(first_low, (M // NB, 1))
    tiled_two = jnp.tile(second_low, (M // NB, 1))
    first_panel = jnp.where(row_bid[:, None] > 0, first_solve, jnp.where(row_bid[:, None] == 0, tiled_one, 0.0))
    second_panel = jnp.where(row_bid[:, None] > 1, second_solve, jnp.where(row_bid[:, None] == 1, tiled_two, 0.0))

    def one_block(slot_id):
        start = slot_id * NB
        values = lax.dynamic_slice_in_dim(kernel, start, NB)
        values = values - product(lax.dynamic_slice_in_dim(first_used, start, NB), first_cols)
        values = values - product(lax.dynamic_slice_in_dim(second_used, start, NB), second_cols)
        values = values.at[:, 0:NB].set(lax.dynamic_slice_in_dim(first_panel, start, NB))
        values = values.at[:, cols_dev:cols_dev + NB].set(lax.dynamic_slice_in_dim(second_panel, start, NB))
        row_blk = lax.dynamic_index_in_dim(row_bid, start, keepdims=False)
        return jnp.where((row_blk < 2) & (col_bid[None, :] > row_blk), 0.0, values)
    return lax.map(one_block, jnp.arange(M // NB, dtype=jnp.int32)).reshape(M, M)
```

```python
import jax
import jax.numpy as jnp
from jax import lax
from jax.experimental import pallas as pl
from jax.experimental.pallas import tpu as pltpu
from jax.sharding import PartitionSpec as P

NB = 256
F32 = jnp.float32
MESH = pl.DeviceIdType.MESH
HI = lax.Precision.HIGHEST

CH = 64
PC_N = 512 // CH
D_N = NB // CH
R_N = 2 * PC_N
LAG = 2
ZP, ZM, YP, YM, XP, XM, PA = range(7)


def dot(a, b, ca=1, cb=0):
    return lax.dot_general(
        a, b, (((ca,), (cb,)), ((), ())), precision=HI, preferred_element_type=F32
    )


def comm_kernel(
    a, pc, rr, dd, head, headt, dsend, drecv, psend, precv, zsend, zrecv, ysend, yrecv, lsem
):
    row = lax.axis_index("row")
    col = lax.axis_index("col")
    x, k = row // 2, row % 2
    y, z = col // 8, col % 8

    def at(nx, ny, nz, nk):
        return ((nx % 4) * 2 + nk, (ny % 4) * 8 + nz % 8)

    near = {
        ZP: at(x, y, z + 1, k),
        ZM: at(x, y, z + 7, k),
        YP: at(x, y + 1, z, k),
        YM: at(x, y + 3, z, k),
        XP: at(x + 1, y, z, k),
        XM: at(x + 3, y, z, k),
        PA: at(x, y, z, 1 - k),
    }
    barrier = pltpu.get_barrier_semaphore()
    for target in near.values():
        pl.semaphore_signal(barrier, inc=1, device_id=target, device_id_type=MESH)

    def remote(src, dst, send, recv, way):
        return pltpu.make_async_remote_copy(
            src_ref=src, dst_ref=dst, send_sem=send, recv_sem=recv,
            device_id=near[way], device_id_type=MESH,
        )

    load = pltpu.make_async_copy(a.at[pl.ds(0, NB), :], head, lsem.at[0])
    load.start()
    load.wait()
    headt[...] = head[...].T
    fill = pltpu.make_async_copy(headt, pc.at[k], lsem.at[1])

    @pl.when(x == 0)
    def _():
        fill.start()
        fill.wait()

    roots = ((0, 0), (0, 1), (1, 1))
    for i, (dk, dz0) in enumerate(roots):
        @pl.when((x == 0) & (y == 0) & (z == dz0) & (k == dk))
        def _():
            own = pltpu.make_async_copy(a.at[pl.ds(0, NB), pl.ds(0, NB)], dd.at[i], lsem.at[2])
            own.start()
            own.wait()

    pl.semaphore_wait(barrier, 7)

    def d_ways(i):
        dk, dz0 = roots[i]
        dz = (z + 8 - dz0) % 8
        line = (x == 0) & (y == 0)
        return (
            (ZP, line & (dz <= 3)),
            (ZM, line & ((dz == 0) | (dz >= 6))),
            (YP, (x == 0) & (y <= 1)),
            (YM, (x == 0) & (y == 0)),
            (XP, x <= 1),
            (XM, x == 0),
            (PA, x >= 0),
        )

    def d_copy(i, t, way):
        part = dd.at[i, pl.ds(pl.multiple_of(t * CH, CH), CH), :]
        return remote(part, part, dsend.at[way, i, t], drecv.at[i, t], way)

    def d_all():
        for i, (dk, dz0) in enumerate(roots):
            def step(t, carry):
                root = (x == 0) & (y == 0) & (z == dz0) & (k == dk)

                @pl.when(jnp.logical_not(root))
                def _():
                    d_copy(i, t, PA).wait_recv()

                for way, goes in d_ways(i):
                    @pl.when(goes & (k == dk))
                    def _():
                        d_copy(i, t, way).start()
                return carry
            lax.fori_loop(0, D_N, step, 0)

    def d_end():
        for i, (dk, dz0) in enumerate(roots):
            def step(t, carry):
                for way, goes in d_ways(i):
                    @pl.when(goes & (k == dk))
                    def _():
                        d_copy(i, t, way).wait_send()
                return carry
            lax.fori_loop(0, D_N, step, 0)

    p_ways = ((XP, x <= 1), (XM, x == 0), (PA, x >= 0))

    def p_copy(kk, t, way):
        part = pc.at[kk, pl.ds(pl.multiple_of(t * CH, CH), CH), :]
        return remote(part, part, psend.at[way - XP, t], precv.at[kk, t], way)

    def p_step(t):
        @pl.when(x > 0)
        def _():
            p_copy(k, t, XP).wait_recv()
        for way, goes in p_ways:
            @pl.when(goes)
            def _():
                p_copy(k, t, way).start()

    @pl.when(x == 0)
    def _():
        def step(t, carry):
            p_step(t)
            return carry
        lax.fori_loop(0, PC_N, step, 0)
        d_all()

    dz = (z + 8 - row) % 8
    source = dz == 0
    z_ways = ((ZP, dz <= 3), (ZM, source | (dz >= 6)))

    def r_part(ny, t):
        kk = (k + t // PC_N) % 2
        return rr.at[ny % 4, kk, pl.ds(pl.multiple_of((t % PC_N) * CH, CH), CH), :]

    def z_copy(t, way):
        return remote(r_part(y, t), r_part(y, t), zsend.at[way, t], zrecv.at[t], way)

    def y_copy(ny, t, way):
        slot = 0 if ny is y else 1
        return remote(
            r_part(ny, t), r_part(ny, t), ysend.at[way - YP, slot, t], yrecv.at[way - YP, slot, t],
            way,
        )

    def r_step(t):
        @pl.when(source)
        def _():
            @pl.when(t >= PC_N)
            def _():
                p_copy(1 - k, t - PC_N, PA).wait_recv()
            kk = (k + t // PC_N) % 2
            own = pltpu.make_async_copy(
                pc.at[kk, pl.ds(pl.multiple_of((t % PC_N) * CH, CH), CH), :],
                r_part(y, t), lsem.at[3],
            )
            own.start()
            own.wait()

        @pl.when(jnp.logical_not(source))
        def _():
            z_copy(t, ZP).wait_recv()
        for way, goes in z_ways:
            @pl.when(goes)
            def _():
                z_copy(t, way).start()
        y_copy(y, t, YP).start()
        y_copy(y, t, YM).start()

    def ring_step(t):
        below, above = y + 3, y + 1
        remote(r_part(below, t), r_part(below, t), ysend.at[0, 0, t], yrecv.at[0, 0, t], YP).wait_recv()
        remote(r_part(above, t), r_part(above, t), ysend.at[1, 0, t], yrecv.at[1, 0, t], YM).wait_recv()

        @pl.when(t % 2 == 0)
        def _():
            y_copy(below, t, YP).start()

        @pl.when(t % 2 == 1)
        def _():
            y_copy(above, t, YM).start()

    def main(t, carry):
        @pl.when((x > 0) & (t < PC_N))
        def _():
            p_step(t)

        @pl.when(t < R_N)
        def _():
            r_step(t)

        @pl.when(t >= LAG)
        def _():
            ring_step(t - LAG)
        return carry
    lax.fori_loop(0, R_N + LAG, main, 0)

    @pl.when(x > 0)
    def _():
        d_all()

    def finish(t, carry):
        across = y + 2

        @pl.when(t % 2 == 0)
        def _():
            y_copy(across, t, YP).wait_recv()
            y_copy(across, t, YP).wait_send()

        @pl.when(t % 2 == 1)
        def _():
            y_copy(across, t, YM).wait_recv()
            y_copy(across, t, YM).wait_send()
        y_copy(y, t, YP).wait_send()
        y_copy(y, t, YM).wait_send()
        for way, goes in z_ways:
            @pl.when(goes)
            def _():
                z_copy(t, way).wait_send()

        @pl.when(t < PC_N)
        def _():
            @pl.when(jnp.logical_not(source))
            def _():
                p_copy(1 - k, t, PA).wait_recv()
            for way, goes in p_ways:
                @pl.when(goes)
                def _():
                    p_copy(k, t, way).wait_send()
        return carry
    lax.fori_loop(0, R_N, finish, 0)
    d_end()


def gather(kernel):
    vmem = pl.BlockSpec(memory_space=pltpu.VMEM)
    dma = pltpu.SemaphoreType.DMA
    return pl.pallas_call(
        comm_kernel,
        out_shape=(
            jax.ShapeDtypeStruct((2, 512, NB), F32),
            jax.ShapeDtypeStruct((4, 2, 512, NB), F32),
            jax.ShapeDtypeStruct((3, NB, NB), F32),
        ),
        in_specs=[pl.BlockSpec(memory_space=pl.ANY)],
        out_specs=(vmem, vmem, vmem),
        scratch_shapes=[
            pltpu.VMEM((NB, 512), F32),
            pltpu.VMEM((512, NB), F32),
            dma((7, 3, D_N)),
            dma((3, D_N)),
            dma((3, PC_N)),
            dma((2, PC_N)),
            dma((2, R_N)),
            dma((R_N,)),
            dma((2, 2, R_N)),
            dma((2, 2, R_N)),
            dma((4,)),
        ],
        compiler_params=pltpu.CompilerParams(
            collective_id=0, has_side_effects=True, vmem_limit_bytes=32 << 20
        ),
        name="gather_panels",
    )(kernel)


def factor_slabs(fac):
    rows = lax.broadcasted_iota(jnp.int32, (8, 128), 0)
    for i in range(16):
        lo = 8 * i
        left = fac[lo : lo + 8, 0:128]
        right = fac[lo : lo + 8, 128:256]
        cols = [jnp.broadcast_to(left[:, lo + q : lo + q + 1], (8, 128)) for q in range(8)]
        for q in range(8):
            pivot = jnp.broadcast_to(cols[q][q : q + 1, :], (8, 128))
            inv = lax.rsqrt(pivot)
            coef = jnp.where(rows > q, cols[q] * inv, 0.0)
            scale = jnp.where(rows == q, inv, 1.0)
            u_left = jnp.broadcast_to(left[q : q + 1, :], (8, 128)) * inv
            u_right = jnp.broadcast_to(right[q : q + 1, :], (8, 128)) * inv
            left = left * scale - coef * u_left
            right = right * scale - coef * u_right
            for m in range(q + 1, 8):
                head = jnp.broadcast_to(cols[m][q : q + 1, :], (8, 128)) * inv
                cols[m] = cols[m] - coef * head
        fac[lo : lo + 8, 128:256] = right
        if i < 15:
            low = lo + 8
            wide = jnp.concatenate([left, right], axis=1)
            fac[low:128, :] = fac[low:128, :] - dot(left, wide, 0, 0)[low:128, :]


def factor_kernel(dd, pc, gt, low, mat, fac):
    col = lax.axis_index("col")
    ident = (
        lax.broadcasted_iota(jnp.int32, (128, 128), 0)
        == lax.broadcasted_iota(jnp.int32, (128, 128), 1)
    ).astype(F32)
    mat[...] = jnp.zeros_like(mat)
    for b in range(4):
        half, off = b // 2, b % 2 * 128
        mat[b, :, half * 256 : half * 256 + 256] = dd[2 * half, off : off + 128, :]
        if half == 0:
            mat[b, :, 256:512] = dd[1, off : off + 128, :]
        mat[b, :, 512 + 128 * b : 640 + 128 * b] = ident

    def block(b, carry):
        fac[:, 0:128] = mat[b, :, pl.ds(pl.multiple_of(b * 128, 128), 128)]
        fac[:, 128:256] = ident
        factor_slabs(fac)
        panel = dot(fac[:, 128:256], mat[b])
        mat[b] = panel

        def trail(i, c2):
            lhs = mat[b, :, pl.ds(pl.multiple_of(i * 128, 128), 128)]
            mat[i] = mat[i] - dot(lhs, mat[b], 0, 0)
            return c2
        lax.fori_loop(b + 1, 4, trail, 0)
        return carry
    lax.fori_loop(0, 4, block, 0)

    wide = mat[...].reshape(512, 1024)
    upper = wide[:, 0:512]
    winv = wide[:, 512:1024]
    tri = lax.broadcasted_iota(jnp.int32, (NB, NB), 0) >= lax.broadcasted_iota(jnp.int32, (NB, NB), 1)
    low[0] = jnp.where(tri, upper[0:256, 0:256].T, 0.0)
    low[1] = jnp.where(tri, upper[256:512, 256:512].T, 0.0)
    solved = dot(winv[:, 0:256], pc[0], 1, 1) + dot(winv[:, 256:512], pc[1], 1, 1)
    gt[...] = dot(winv, solved, 0, 0)

    @pl.when(col == 0)
    def _():
        gt[:, 0:256] = -winv[0:256, :].T

    @pl.when(col == 1)
    def _():
        gt[:, 0:256] = -winv[256:512, :].T


def factor(dd, pc):
    return pl.pallas_call(
        factor_kernel,
        out_shape=(
            jax.ShapeDtypeStruct((512, 512), F32),
            jax.ShapeDtypeStruct((2, NB, NB), F32),
        ),
        scratch_shapes=[pltpu.VMEM((4, 128, 1024), F32), pltpu.VMEM((128, 256), F32)],
        compiler_params=pltpu.CompilerParams(vmem_limit_bytes=48 << 20),
        name="factor_diagonal",
    )(dd, pc)


def update_kernel(a, rr, gt, low, out):
    row = lax.axis_index("row")
    col = lax.axis_index("col")
    slot = pl.program_id(0)
    acc = dot(rr[0, 0], gt[0:256, :]) + dot(rr[0, 1], gt[256:512, :])
    panel = (lax.broadcasted_iota(jnp.int32, (NB, 512), 1) < NB) & (col < 2)
    out[...] = jnp.where(panel, 0.0, a[...]) - acc

    @pl.when((slot == 0) & (row < 2))
    def _():
        out[:, 256:512] = jnp.zeros((NB, NB), F32)

        @pl.when(row == col)
        def _():
            out[:, 0:256] = low[row]

        @pl.when((col > 1) | ((row == 0) & (col == 1)))
        def _():
            out[:, 0:256] = jnp.zeros((NB, NB), F32)


def update(kernel, rr, gt, low):
    return pl.pallas_call(
        update_kernel,
        out_shape=jax.ShapeDtypeStruct(kernel.shape, F32),
        grid=(8,),
        in_specs=[
            pl.BlockSpec((NB, 512), lambda j: (j, 0)),
            pl.BlockSpec((1, 2, NB, NB), lambda j: (j % 4, 0, j // 4, 0)),
            pl.BlockSpec((512, 512), lambda j: (0, 0)),
            pl.BlockSpec((2, NB, NB), lambda j: (0, 0, 0)),
        ],
        out_specs=pl.BlockSpec((NB, 512), lambda j: (j, 0)),
        compiler_params=pltpu.CompilerParams(vmem_limit_bytes=48 << 20),
        name="update_trailing",
    )(kernel, rr, gt, low)


def local(kernel):
    pc, rr, dd = gather(kernel)
    gt, low = factor(dd, pc)
    return update(kernel, rr, gt, low)


def solution(mesh):
    placed = (P("row", "col"),)
    return jax.shard_map(
        local, mesh=mesh, in_specs=placed, out_specs=P("row", "col"), check_vma=False
    )
```

```python
import jax
import jax.numpy as jnp
from jax import lax
from jax.experimental import pallas as pl
from jax.experimental.pallas import tpu as pltpu
from jax.sharding import PartitionSpec as P

NB = 256
F32 = jnp.float32
MESH = pl.DeviceIdType.MESH
HI = lax.Precision.HIGHEST

CH = 64
DH = 32
PC_N = 512 // CH
R_N = 2 * PC_N
D_N = NB // DH
LAG = 2
ZP, ZM, YP, YM, XP, XM, PA = range(7)


def dot(a, b, ca=1, cb=0):
    return lax.dot_general(
        a, b, (((ca,), (cb,)), ((), ())), precision=HI, preferred_element_type=F32
    )


def main_kernel(
    a, rr, gl, pc, oth, dd, head, headt, mat, fac,
    dsend, drecv, psend, precv, zsend, zrecv, ysend, yrecv, osend, orecv, gsend, grecv, lsem,
):
    row = lax.axis_index("row")
    col = lax.axis_index("col")
    x, k = row // 2, row % 2
    y, z = col // 8, col % 8

    def at(nx, ny, nz, nk):
        return ((nx % 4) * 2 + nk, (ny % 4) * 8 + nz % 8)

    near = {
        ZP: at(x, y, z + 1, 1),
        ZM: at(x, y, z + 7, 1),
        YP: at(x, y + 1, z, 1),
        YM: at(x, y + 3, z, 1),
        XP: at(x + 1, y, z, 1),
        XM: at(x + 3, y, z, 1),
        PA: at(x, y, z, 1 - k),
    }
    barrier = pltpu.get_barrier_semaphore()

    def greet(target):
        pl.semaphore_signal(barrier, inc=1, device_id=target, device_id_type=MESH)

    for way in (XP, XM, PA):
        greet(near[way])

    @pl.when(k == 1)
    def _():
        for way in (ZP, ZM, YP, YM):
            greet(near[way])
        greet(at(x + 1, y, z, 0))
        greet(at(x + 3, y, z, 0))

    def remote(src, dst, send, recv, way):
        return pltpu.make_async_remote_copy(
            src_ref=src, dst_ref=dst, send_sem=send, recv_sem=recv,
            device_id=near[way], device_id_type=MESH,
        )

    def rows_of(t, size):
        return pl.ds(pl.multiple_of(t * size, size), size)

    @pl.when(x == 0)
    def _():
        load = pltpu.make_async_copy(a.at[pl.ds(0, NB), :], head, lsem.at[0])
        load.start()
        load.wait()
        headt[...] = head[...].T

    @pl.when((x == 0) & (y == 0) & (z < 2) & ((k == 0) | (z == 1)))
    def _():
        own = pltpu.make_async_copy(
            a.at[pl.ds(0, NB), pl.ds(0, NB)], dd.at[z + k], lsem.at[1]
        )
        own.start()
        own.wait()

    def d_root(i):
        return (x == 0) & (y == 0) & (z == jnp.minimum(i, 1))

    def d_ways(i):
        dz = (z + 8 - jnp.minimum(i, 1)) % 8
        line = (x == 0) & (y == 0)
        return (
            (ZP, line & (dz <= 3)),
            (ZM, line & ((dz == 0) | (dz >= 6))),
            (YP, (x == 0) & (y <= 1)),
            (YM, (x == 0) & (y == 0)),
            (XP, x <= 1),
            (XM, x == 0),
            (PA, jnp.logical_not(d_root(i) & (i < 2))),
        )

    def d_copy(i, t, way):
        part = dd.at[i, rows_of(t, DH), :]
        return remote(part, part, dsend.at[way, i, t], drecv.at[i, t], way)

    def d_step(u):
        i, t = u // D_N, u % D_N

        @pl.when(jnp.logical_not(d_root(i) & (i == 2)))
        def _():
            d_copy(i, t, PA).wait_recv()

        for way, goes in d_ways(i):
            @pl.when(goes)
            def _():
                d_copy(i, t, way).start()

    def p_copy(kk, t, way):
        part = pc.at[kk, rows_of(t, CH), :]
        return remote(part, part, psend.at[way - XP, kk, t], precv.at[kk, t], way)

    def p_first(t, way):
        return remote(
            headt.at[rows_of(t, CH), :], pc.at[k, rows_of(t, CH), :],
            psend.at[way - XP, k, t], precv.at[k, t], way,
        )

    def fill_own():
        return pltpu.make_async_copy(headt, pc.at[k], lsem.at[2])

    def p_step(kk, t):
        p_copy(kk, t, XP).wait_recv()

        @pl.when(x == 1)
        def _():
            p_copy(kk, t, XP).start()
        p_copy(kk, t, PA).start()

    def held(g):
        return rr if g else oth

    def source(g):
        return z == 2 * x + g

    def z_ways(g):
        dz = (z + 8 - 2 * x - g) % 8
        return ((ZP, dz <= 3), (ZM, (dz == 0) | (dz >= 6)))

    def r_part(buf, ny, t):
        return buf.at[ny % 4, t % 2, rows_of(t // 2, CH), :]

    def z_copy(g, t, way):
        part = r_part(held(g), y, t)
        return remote(part, part, zsend.at[way, g, t], zrecv.at[g, t], way)

    def y_copy(g, ny, t, way, slot):
        part = r_part(held(g), ny, t)
        return remote(
            part, part, ysend.at[way - YP, slot, g, t], yrecv.at[way - YP, slot, g, t], way
        )

    def o_copy(ny, t):
        ny = ny % 4
        return remote(
            r_part(oth, ny, t), r_part(rr, ny, t), osend.at[ny, t], orecv.at[ny, t], PA
        )

    def r_step(g, t):
        @pl.when(source(g))
        def _():
            own = pltpu.make_async_copy(
                pc.at[t % 2, rows_of(t // 2, CH), :], r_part(held(g), y, t), lsem.at[3]
            )
            own.start()
            own.wait()

        @pl.when(jnp.logical_not(source(g)))
        def _():
            z_copy(g, t, ZP).wait_recv()
        for way, goes in z_ways(g):
            @pl.when(goes)
            def _():
                z_copy(g, t, way).start()
        y_copy(g, y, t, YP, 0).start()
        y_copy(g, y, t, YM, 0).start()
        if g == 0:
            o_copy(y, t).start()

    def ring_step(g, t):
        y_copy(g, y + 3, t, YP, 0).wait_recv()
        y_copy(g, y + 1, t, YM, 0).wait_recv()

        @pl.when(t // 2 % 2 == 0)
        def _():
            y_copy(g, y + 3, t, YP, 1).start()

        @pl.when(t // 2 % 2 == 1)
        def _():
            y_copy(g, y + 1, t, YM, 1).start()
        if g == 0:
            o_copy(y + 3, t).start()
            o_copy(y + 1, t).start()

    def last_step(g, t):
        @pl.when(t // 2 % 2 == 0)
        def _():
            y_copy(g, y + 2, t, YP, 1).wait_recv()

        @pl.when(t // 2 % 2 == 1)
        def _():
            y_copy(g, y + 2, t, YM, 1).wait_recv()
        if g == 0:
            o_copy(y + 2, t).start()

    def loop(n, body):
        def step(t, carry):
            body(t)
            return carry
        lax.fori_loop(0, n, step, 0)

    def g_copy(h):
        part = gl.at[pl.ds(256 * h, 256), :]
        return remote(part, part, gsend.at[h], grecv.at[h], PA)

    @pl.when(k == 1)
    def _carry():
        pl.semaphore_wait(barrier, 9)

        @pl.when(x == 0)
        def _():
            fill_own().start()

            def first(t):
                for way in (XP, XM, PA):
                    p_first(t, way).start()
            loop(PC_N, first)
            fill_own().wait()
            loop(3 * D_N, d_step)

        begin = jnp.where(x == 2, 4, 1)

        def body(t):
            @pl.when(t < R_N)
            def _():
                @pl.when(x > 0)
                def _():
                    p_step(t % 2, t // 2)

                @pl.when((x == 0) & (t % 2 == 0))
                def _():
                    p_copy(0, t // 2, PA).wait_recv()
                r_step(0, t)
                r_step(1, t)

            @pl.when((x > 0) & (t >= begin) & (t < begin + 6))
            def _():
                def four(q):
                    d_step(4 * (t - begin) + q)
                loop(4, four)

            @pl.when(t >= LAG)
            def _():
                ring_step(0, t - LAG)
                ring_step(1, t - LAG)

            @pl.when(t >= 2 * LAG)
            def _():
                last_step(0, t - 2 * LAG)
                last_step(1, t - 2 * LAG)
        def guarded(t):
            @pl.when(t < R_N + LAG)
            def _():
                body(t)

            @pl.when(t >= R_N + LAG)
            def _():
                last_step(0, t - 2 * LAG)
                last_step(1, t - 2 * LAG)
        loop(R_N + 2 * LAG, guarded)

        def finish(t):
            for g in range(2):
                for way, goes in z_ways(g):
                    @pl.when(goes)
                    def _():
                        z_copy(g, t, way).wait_send()
                y_copy(g, y, t, YP, 0).wait_send()
                y_copy(g, y, t, YM, 0).wait_send()

                @pl.when(t // 2 % 2 == 0)
                def _():
                    y_copy(g, y + 3, t, YP, 1).wait_send()

                @pl.when(t // 2 % 2 == 1)
                def _():
                    y_copy(g, y + 1, t, YM, 1).wait_send()
            for q in range(4):
                o_copy(y + q, t).wait_send()

            @pl.when(x == 0)
            def _():
                @pl.when(t < PC_N)
                def _():
                    for way in (XP, XM, PA):
                        p_first(t, way).wait_send()

            @pl.when(x == 1)
            def _():
                p_copy(t % 2, t // 2, XP).wait_send()

            @pl.when(x > 0)
            def _():
                p_copy(t % 2, t // 2, PA).wait_send()
        loop(R_N, finish)

        def d_end(u):
            i, t = u // D_N, u % D_N
            for way, goes in d_ways(i):
                @pl.when(goes)
                def _():
                    d_copy(i, t, way).wait_send()
        loop(3 * D_N, d_end)
        for h in range(3):
            g_copy(h).wait_recv()

    @pl.when(k == 0)
    def _factor():
        pl.semaphore_wait(barrier, 3)
        mine = (x == 0) & (y == 0) & (z < 2)

        @pl.when(mine)
        def _():
            def send(t):
                d_copy(z, t, PA).start()
            loop(D_N, send)

        @pl.when(x == 0)
        def _():
            def first(t):
                for way in (PA, XP, XM):
                    p_first(t, way).start()
            loop(PC_N, first)
            fill_own().start()

        def d_wait(i):
            @pl.when(jnp.logical_not(d_root(i) & (i < 2)))
            def _():
                def one(t):
                    d_copy(i, t, PA).wait_recv()
                loop(D_N, one)

        def panel_wait():
            @pl.when(x == 0)
            def _():
                fill_own().wait()

            @pl.when(x > 0)
            def _():
                def one(t):
                    p_copy(0, t, PA).wait_recv()
                loop(PC_N, one)

            def other(t):
                p_copy(1, t, PA).wait_recv()
            loop(PC_N, other)

        factor(dd, pc, gl, mat, fac, col, d_wait, panel_wait, lambda h: g_copy(h).start())

        def rest(t):
            for q in range(4):
                o_copy(q, t).wait_recv()
        loop(R_N, rest)

        @pl.when(mine)
        def _():
            def sent(t):
                d_copy(z, t, PA).wait_send()
            loop(D_N, sent)

        @pl.when(x == 0)
        def _():
            def sent(t):
                for way in (PA, XP, XM):
                    p_first(t, way).wait_send()
            loop(PC_N, sent)
        for h in range(3):
            g_copy(h).wait_send()


def gather_and_factor(kernel):
    vmem = pl.BlockSpec(memory_space=pltpu.VMEM)
    dma = pltpu.SemaphoreType.DMA
    return pl.pallas_call(
        main_kernel,
        out_shape=(
            jax.ShapeDtypeStruct((4, 2, 512, NB), F32),
            jax.ShapeDtypeStruct((768, 512), F32),
        ),
        in_specs=[pl.BlockSpec(memory_space=pltpu.HBM)],
        out_specs=(vmem, vmem),
        scratch_shapes=[
            pltpu.VMEM((2, 512, NB), F32),
            pltpu.VMEM((4, 2, 512, NB), F32),
            pltpu.VMEM((3, NB, NB), F32),
            pltpu.VMEM((NB, 512), F32),
            pltpu.VMEM((512, NB), F32),
            pltpu.VMEM((4, 128, 1024), F32),
            pltpu.VMEM((128, 256), F32),
            dma((7, 3, D_N)),
            dma((3, D_N)),
            dma((3, 2, PC_N)),
            dma((2, PC_N)),
            dma((2, 2, R_N)),
            dma((2, R_N)),
            dma((2, 2, 2, R_N)),
            dma((2, 2, 2, R_N)),
            dma((4, R_N)),
            dma((4, R_N)),
            dma((3,)),
            dma((3,)),
            dma((4,)),
        ],
        compiler_params=pltpu.CompilerParams(
            collective_id=0, has_side_effects=True, vmem_limit_bytes=56 << 20
        ),
        name="gather_and_factor",
    )(kernel)


def factor_slabs(fac):
    rows = lax.broadcasted_iota(jnp.int32, (8, 128), 0)
    for i in range(16):
        lo = 8 * i
        left = fac[lo : lo + 8, 0:128]
        right = fac[lo : lo + 8, 128:256]
        cols = [jnp.broadcast_to(left[:, lo + q : lo + q + 1], (8, 128)) for q in range(8)]
        for q in range(8):
            pivot = jnp.broadcast_to(cols[q][q : q + 1, :], (8, 128))
            inv = lax.rsqrt(pivot)
            coef = jnp.where(rows > q, cols[q] * inv, 0.0)
            scale = jnp.where(rows == q, inv, 1.0)
            u_left = jnp.broadcast_to(left[q : q + 1, :], (8, 128)) * inv
            u_right = jnp.broadcast_to(right[q : q + 1, :], (8, 128)) * inv
            left = left * scale - coef * u_left
            right = right * scale - coef * u_right
            for m in range(q + 1, 8):
                head = jnp.broadcast_to(cols[m][q : q + 1, :], (8, 128)) * inv
                cols[m] = cols[m] - coef * head
        fac[lo : lo + 8, 128:256] = right
        if i < 15:
            low = lo + 8
            wide = jnp.concatenate([left, right], axis=1)
            fac[low:128, :] = fac[low:128, :] - dot(left, wide, 0, 0)[low:128, :]


def factor(dd, pc, gl, mat, fac, col, d_wait, panel_wait, send):
    ident = (
        lax.broadcasted_iota(jnp.int32, (128, 128), 0)
        == lax.broadcasted_iota(jnp.int32, (128, 128), 1)
    ).astype(F32)
    mat[...] = jnp.zeros_like(mat)
    for b in range(4):
        mat[b, :, 512 + 128 * b : 640 + 128 * b] = ident
    d_wait(0)
    for b in range(2):
        mat[b, :, 0:256] = dd[0, 128 * b : 128 * b + 128, :]

    def block(b, carry):
        fac[:, 0:128] = mat[b, :, pl.ds(pl.multiple_of(b * 128, 128), 128)]
        fac[:, 128:256] = ident
        factor_slabs(fac)

        @pl.when(b == 0)
        def _():
            d_wait(1)
            d_wait(2)
            for q in range(2):
                mat[q, :, 256:512] = dd[1, 128 * q : 128 * q + 128, :]
                mat[q + 2, :, 256:512] = dd[2, 128 * q : 128 * q + 128, :]
        panel = dot(fac[:, 128:256], mat[b])
        mat[b] = panel

        def trail(i, c2):
            lhs = mat[b, :, pl.ds(pl.multiple_of(i * 128, 128), 128)]
            mat[i] = mat[i] - dot(lhs, mat[b], 0, 0)
            return c2
        lax.fori_loop(b + 1, 4, trail, 0)
        return carry
    lax.fori_loop(0, 4, block, 0)

    wide = mat[...].reshape(512, 1024)
    winv = wide[:, 512:1024]
    tri = lax.broadcasted_iota(jnp.int32, (NB, NB), 0) >= lax.broadcasted_iota(jnp.int32, (NB, NB), 1)
    for h in range(2):
        own = slice(256 * h, 256 * h + 256)
        gl[512:768, own] = jnp.where(tri, wide[own, own].T, 0.0)
    send(2)
    panel_wait()
    solved = dot(winv[:, 0:256], pc[0], 1, 1) + dot(winv[:, 256:512], pc[1], 1, 1)
    for h in range(2):
        rows = slice(256 * h, 256 * h + 256)
        gl[rows, :] = dot(winv[:, rows], solved, 0, 0)
        for q in range(2):
            @pl.when(col == q)
            def _():
                gl[rows, 0:256] = -winv[256 * q : 256 * q + 256, rows].T
        send(h)


def update_kernel(a, rr, gl, out, hi, lo):
    row = lax.axis_index("row")
    col = lax.axis_index("col")
    slot = pl.program_id(0)

    @pl.when(slot == 0)
    def _():
        g = gl[0:512, :]
        top = g.astype(jnp.bfloat16)
        hi[...] = top
        lo[...] = (g - top.astype(F32)).astype(jnp.bfloat16)

    def mul(p, q):
        return jnp.dot(p, q, preferred_element_type=F32)

    acc = jnp.zeros((NB, 512), F32)
    for kk in range(2):
        r = rr[slot % 4, kk, pl.ds(pl.multiple_of(slot // 4 * NB, NB), NB), :]
        top = r.astype(jnp.bfloat16)
        rest = (r - top.astype(F32)).astype(jnp.bfloat16)
        rows = slice(kk * NB, kk * NB + NB)
        acc = acc + mul(top, hi[rows, :]) + (mul(top, lo[rows, :]) + mul(rest, hi[rows, :]))
    panel = (lax.broadcasted_iota(jnp.int32, (NB, 512), 1) < NB) & (col < 2)
    out[...] = jnp.where(panel, 0.0, a[...]) - acc

    @pl.when((slot == 0) & (row < 2))
    def _():
        out[:, 256:512] = jnp.zeros((NB, NB), F32)
        for q in range(2):
            @pl.when((row == q) & (col == q))
            def _():
                out[:, 0:256] = gl[512:768, 256 * q : 256 * q + 256]

        @pl.when((col > 1) | ((row == 0) & (col == 1)))
        def _():
            out[:, 0:256] = jnp.zeros((NB, NB), F32)


def update(kernel, rr, gl):
    vmem = pl.BlockSpec(memory_space=pltpu.VMEM)
    return pl.pallas_call(
        update_kernel,
        out_shape=jax.ShapeDtypeStruct(kernel.shape, F32),
        grid=(8,),
        in_specs=[pl.BlockSpec((NB, 512), lambda j: (j, 0)), vmem, vmem],
        out_specs=pl.BlockSpec((NB, 512), lambda j: (j, 0)),
        scratch_shapes=[pltpu.VMEM((512, 512), jnp.bfloat16)] * 2,
        compiler_params=pltpu.CompilerParams(vmem_limit_bytes=24 << 20),
        name="update_trailing",
    )(kernel, rr, gl)


def local(kernel):
    rr, gl = gather_and_factor(kernel)
    return update(kernel, rr, gl)


def solution(mesh):
    placed = (P("row", "col"),)
    return jax.shard_map(
        local, mesh=mesh, in_specs=placed, out_specs=P("row", "col"), check_vma=False
    )
```

```python
import jax
import jax.numpy as jnp
from jax import lax
from jax.experimental import pallas as pl
from jax.experimental.pallas import tpu as pltpu
from jax.sharding import PartitionSpec as P

NB = 256
F32 = jnp.float32
MESH = pl.DeviceIdType.MESH
HI = lax.Precision.HIGHEST

CH = 64
DH = 32
PC_N = 512 // CH
D_N = NB // DH
LAGS = (0, 1, 2, 3)
ZP, ZM, YP, YM, XP, XM, PA, CP, CM = range(9)


def dot(a, b, ca=1, cb=0):
    return lax.dot_general(
        a, b, (((ca,), (cb,)), ((), ())), precision=HI, preferred_element_type=F32
    )


def main_kernel(
    a, rr, gl, pc, oth, dd, head, headt, mat, fac,
    dsend, drecv, psend, precv, ppass, zsend, zrecv, ysend, yrecv,
    osend, orecv, gsend, grecv, lsem,
):
    row = lax.axis_index("row")
    col = lax.axis_index("col")
    x, k = row // 2, row % 2
    y, z = col // 8, col % 8

    def at(nx, ny, nz, nk):
        return ((nx % 4) * 2 + nk, (ny % 4) * 8 + nz % 8)

    near = {
        ZP: at(x, y, z + 1, k),
        ZM: at(x, y, z + 7, k),
        YP: at(x, y + 1, z, k),
        YM: at(x, y + 3, z, k),
        XP: at(x + 1, y, z, k),
        XM: at(x + 3, y, z, k),
        PA: at(x, y, z, 1 - k),
        CP: at(x + 1, y, z, 1),
        CM: at(x + 3, y, z, 1),
    }
    barrier = pltpu.get_barrier_semaphore()
    for target in [near[way] for way in range(7)] + [
        at(x + 1, y, z, 1 - k), at(x + 3, y, z, 1 - k)
    ]:
        pl.semaphore_signal(barrier, inc=1, device_id=target, device_id_type=MESH)

    def remote(src, dst, send, recv, way):
        return pltpu.make_async_remote_copy(
            src_ref=src, dst_ref=dst, send_sem=send, recv_sem=recv,
            device_id=near[way], device_id_type=MESH,
        )

    def rows_of(t, size):
        return pl.ds(pl.multiple_of(t * size, size), size)

    @pl.when(x == 0)
    def _():
        load = pltpu.make_async_copy(a.at[pl.ds(0, NB), :], head, lsem.at[0])
        load.start()
        load.wait()
        headt[...] = head[...].T

    @pl.when((x == 0) & (y == 0) & (z < 2) & ((k == 0) | (z == 1)))
    def _():
        own = pltpu.make_async_copy(
            a.at[pl.ds(0, NB), pl.ds(0, NB)], dd.at[z + k], lsem.at[1]
        )
        own.start()
        own.wait()

    below, above, across = (y + 3) % 4, (y + 1) % 4, (y + 2) % 4

    def loop(n, body, first=0):
        def step(t, carry):
            body(t)
            return carry
        lax.fori_loop(first, n, step, 0)

    d_root, d_ways = [], []
    for i in range(3):
        dz = (z + 8 - min(i, 1)) % 8
        line = (x == 0) & (y == 0)
        root = line & (dz == 0)
        d_root.append(root)
        d_ways.append((
            (ZP, line & (dz <= 3)),
            (ZM, line & ((dz == 0) | (dz >= 6))),
            (YP, (x == 0) & (y <= 1)),
            (YM, (x == 0) & (y == 0)),
            (XP, x <= 1),
            (XM, x == 0),
        ))

    def d_copy(i, t, way):
        part = dd.at[i, rows_of(t, DH), :]
        return remote(part, part, dsend.at[way, i], drecv.at[i, t], way)

    def d_whole(i, way):
        return remote(dd.at[i], dd.at[i], dsend.at[way, i], drecv.at[i, 0], way)

    def d_block(i):
        def one(t):
            if i == 2:
                d_copy(i, t, PA).wait_recv()
            else:
                @pl.when(jnp.logical_not(d_root[i]))
                def _():
                    d_copy(i, t, PA).wait_recv()

            for way, goes in d_ways[i]:
                @pl.when(goes)
                def _():
                    d_copy(i, t, way).start()
        loop(D_N, one)

    def p_copy(kk, t, way):
        part = pc.at[kk, rows_of(t, CH), :]
        return remote(part, part, psend.at[way - PA, kk], precv.at[kk, t], way)

    def p_pass(kk, t):
        part = pc.at[kk, rows_of(t, CH), :]
        return remote(part, part, psend.at[0, kk], ppass.at[kk], PA)

    def p_whole(kk, way):
        return remote(pc.at[kk], pc.at[kk], psend.at[way - PA, kk], ppass.at[kk], way)

    def p_first(kk, t, way):
        recv = ppass.at[kk] if (way == PA and kk == 1) else precv.at[kk, t]
        return remote(
            headt.at[rows_of(t, CH), :], pc.at[kk, rows_of(t, CH), :],
            psend.at[way - PA, kk], recv, way,
        )

    def fill_own(kk):
        return pltpu.make_async_copy(headt, pc.at[kk], lsem.at[2])

    def p_step(kk, t):
        p_copy(kk, t, PA).wait_recv()

        @pl.when(x == 1)
        def _():
            p_copy(kk, t, CP).start()
        p_pass(kk, t).start()

    held = (oth, rr)
    source = [z == 2 * x + g for g in range(2)]
    z_ways = []
    for g in range(2):
        dz = (z + 8 - 2 * x - g) % 8
        z_ways.append(((ZP, dz <= 3), (ZM, (dz == 0) | (dz >= 6))))

    def r_part(buf, ny, kk, t):
        return buf.at[ny, kk, rows_of(t, CH), :]

    def z_copy(g, kk, t, way):
        part = r_part(held[g], y, kk, t)
        return remote(part, part, zsend.at[way, g], zrecv.at[g, kk, t], way)

    def y_copy(g, ny, kk, t, way, slot):
        part = r_part(held[g], ny, kk, t)
        return remote(
            part, part, ysend.at[way - YP, slot, g], yrecv.at[way - YP, slot, g, kk, t], way
        )

    def o_copy(ny, kk, t):
        return remote(
            r_part(oth, ny, kk, t), r_part(rr, ny, kk, t), osend.at[0], orecv.at[0], PA
        )

    def own_step(g, kk, t):
        part = pc.at[kk, rows_of(t, CH), :]
        pltpu.make_async_copy(part, r_part(held[g], y, kk, t), lsem.at[3]).start()
        dst = r_part(held[g], y, kk, t)
        for way in (ZP, ZM):
            remote(part, dst, zsend.at[way, g], zrecv.at[g, kk, t], way).start()
        for way in (YP, YM):
            remote(
                part, dst, ysend.at[way - YP, 0, g], yrecv.at[way - YP, 0, g, kk, t], way
            ).start()
        if g == 0:
            remote(part, r_part(rr, y, kk, t), osend.at[0], orecv.at[0], PA).start()

    def pass_step(g, kk, t):
        z_copy(g, kk, t, ZP).wait_recv()
        for way, goes in z_ways[g]:
            @pl.when(goes)
            def _():
                z_copy(g, kk, t, way).start()
        y_copy(g, y, kk, t, YP, 0).start()
        y_copy(g, y, kk, t, YM, 0).start()
        if g == 0:
            o_copy(y, kk, t).start()

    def ring_step(g, kk, t):
        y_copy(g, below, kk, t, YP, 0).wait_recv()
        y_copy(g, above, kk, t, YM, 0).wait_recv()
        if kk == 0:
            y_copy(g, below, kk, t, YP, 1).start()
        else:
            y_copy(g, above, kk, t, YM, 1).start()
        if g == 0:
            o_copy(below, kk, t).start()
            o_copy(above, kk, t).start()

    def last_step(g, kk, t):
        y_copy(g, across, kk, t, YM if kk else YP, 1).wait_recv()
        if g == 0:
            o_copy(across, kk, t).start()

    def g_copy(h):
        part = gl.at[pl.ds(256 * h, 256), :]
        return remote(part, part, gsend.at[h], grecv.at[h], PA)

    @pl.when(k == 1)
    def _carry():
        pl.semaphore_wait(barrier, 9)

        @pl.when(d_root[2])
        def _():
            loop(D_N, lambda t: d_copy(2, t, PA).start())

        @pl.when(x == 0)
        def _():
            fill_own(1).start()

            def first(t):
                for way in (CP, CM, PA):
                    p_first(1, t, way).start()
            loop(PC_N, first)
            fill_own(1).wait()

        def stage0(t):
            for kk in range(2):
                @pl.when(x > 0)
                def _():
                    p_step(kk, t)
                if kk == 0:
                    @pl.when(x == 0)
                    def _():
                        p_copy(0, t, PA).wait_recv()
                for g in range(2):
                    @pl.when(source[g])
                    def _():
                        own_step(g, kk, t)

        def stage1(t):
            for kk in range(2):
                for g in range(2):
                    @pl.when(jnp.logical_not(source[g]))
                    def _():
                        pass_step(g, kk, t)

        def stage2(t):
            for kk in range(2):
                for g in range(2):
                    ring_step(g, kk, t)

        def stage3(t):
            for kk in range(2):
                for g in range(2):
                    last_step(g, kk, t)

        def body(t):
            for lag, stage in enumerate((stage0, stage1, stage2, stage3)):
                at_t = LAGS[lag]

                @pl.when((t >= at_t) & (t < PC_N + at_t))
                def _():
                    stage(t - at_t)
        loop(PC_N + LAGS[-1], body)

        for g in range(2):
            @pl.when(source[g])
            def _():
                pltpu.make_async_copy(pc, held[g].at[y], lsem.at[3]).wait()
        for g in range(2):
            for way, goes in z_ways[g]:
                @pl.when(goes)
                def _():
                    remote(rr.at[0], rr.at[0], zsend.at[way, g], orecv.at[0], way).wait_send()
            for way in (YP, YM):
                remote(rr.at[0], rr.at[0], ysend.at[way - YP, 0, g], orecv.at[0], way).wait_send()
                half = rr.at[0, 0]
                remote(half, half, ysend.at[way - YP, 1, g], orecv.at[0], way).wait_send()
        remote(oth, rr, osend.at[0], orecv.at[0], PA).wait_send()

        @pl.when(x == 0)
        def _():
            for way in (CP, CM, PA):
                p_whole(1, way).wait_send()

        @pl.when(x > 0)
        def _():
            for kk in range(2):
                @pl.when(x == 1)
                def _():
                    p_whole(kk, CP).wait_send()
                p_whole(kk, PA).wait_send()

        @pl.when(d_root[2])
        def _():
            d_whole(2, PA).wait_send()
        for h in range(3):
            g_copy(h).wait_recv()

    @pl.when(k == 0)
    def _factor():
        pl.semaphore_wait(barrier, 9)

        @pl.when(x == 0)
        def _():
            def first(t):
                for way in (PA, CP, CM):
                    p_first(0, t, way).start()
            loop(PC_N, first)
            fill_own(0).start()
        for i in range(3):
            d_block(i)

        def panel_wait():
            @pl.when(x == 0)
            def _():
                fill_own(0).wait()

            @pl.when(x > 0)
            def _():
                p_whole(0, PA).wait_recv()
            p_whole(1, PA).wait_recv()

        factor(dd, pc, gl, mat, fac, col, panel_wait, lambda h: g_copy(h).start())

        remote(oth, rr, osend.at[0], orecv.at[0], PA).wait_recv()
        for i in range(3):
            for way, goes in d_ways[i]:
                @pl.when(goes)
                def _():
                    d_whole(i, way).wait_send()

        @pl.when(x == 0)
        def _():
            for way in (PA, CP, CM):
                p_whole(0, way).wait_send()
        for h in range(3):
            g_copy(h).wait_send()


def gather_and_factor(kernel):
    vmem = pl.BlockSpec(memory_space=pltpu.VMEM)
    dma = pltpu.SemaphoreType.DMA
    return pl.pallas_call(
        main_kernel,
        out_shape=(
            jax.ShapeDtypeStruct((4, 2, 512, NB), F32),
            jax.ShapeDtypeStruct((768, 512), F32),
        ),
        in_specs=[pl.BlockSpec(memory_space=pltpu.HBM)],
        out_specs=(vmem, vmem),
        scratch_shapes=[
            pltpu.VMEM((2, 512, NB), F32),
            pltpu.VMEM((4, 2, 512, NB), F32),
            pltpu.VMEM((3, NB, NB), F32),
            pltpu.VMEM((NB, 512), F32),
            pltpu.VMEM((512, NB), F32),
            pltpu.VMEM((4, 128, 1024), F32),
            pltpu.VMEM((128, 256), F32),
            dma((7, 3)),
            dma((3, D_N)),
            dma((3, 2)),
            dma((2, PC_N)),
            dma((2,)),
            dma((2, 2)),
            dma((2, 2, PC_N)),
            dma((2, 2, 2)),
            dma((2, 2, 2, 2, PC_N)),
            dma((1,)),
            dma((1,)),
            dma((3,)),
            dma((3,)),
            dma((4,)),
        ],
        compiler_params=pltpu.CompilerParams(
            collective_id=0, has_side_effects=True, vmem_limit_bytes=56 << 20
        ),
        name="gather_and_factor",
    )(kernel)


def factor_slabs(fac):
    rows = lax.broadcasted_iota(jnp.int32, (8, 128), 0)
    for i in range(16):
        lo = 8 * i
        left = fac[lo : lo + 8, 0:128]
        right = fac[lo : lo + 8, 128:256]
        cols = [jnp.broadcast_to(left[:, lo + q : lo + q + 1], (8, 128)) for q in range(8)]
        for q in range(8):
            pivot = jnp.broadcast_to(cols[q][q : q + 1, :], (8, 128))
            inv = lax.rsqrt(pivot)
            coef = jnp.where(rows > q, cols[q] * inv, 0.0)
            scale = jnp.where(rows == q, inv, 1.0)
            u_left = jnp.broadcast_to(left[q : q + 1, :], (8, 128)) * inv
            u_right = jnp.broadcast_to(right[q : q + 1, :], (8, 128)) * inv
            left = left * scale - coef * u_left
            right = right * scale - coef * u_right
            for m in range(q + 1, 8):
                head = jnp.broadcast_to(cols[m][q : q + 1, :], (8, 128)) * inv
                cols[m] = cols[m] - coef * head
        fac[lo : lo + 8, 128:256] = right
        if i < 15:
            low = lo + 8
            wide = jnp.concatenate([left, right], axis=1)
            fac[low:128, :] = fac[low:128, :] - dot(left, wide, 0, 0)[low:128, :]


def factor(dd, pc, gl, mat, fac, col, panel_wait, send):
    ident = (
        lax.broadcasted_iota(jnp.int32, (128, 128), 0)
        == lax.broadcasted_iota(jnp.int32, (128, 128), 1)
    ).astype(F32)
    mat[...] = jnp.zeros_like(mat)
    for b in range(4):
        mat[b, :, 512 + 128 * b : 640 + 128 * b] = ident
    for q in range(2):
        mat[q, :, 0:256] = dd[0, 128 * q : 128 * q + 128, :]
        mat[q, :, 256:512] = dd[1, 128 * q : 128 * q + 128, :]
        mat[q + 2, :, 256:512] = dd[2, 128 * q : 128 * q + 128, :]

    def block(b, carry):
        fac[:, 0:128] = mat[b, :, pl.ds(pl.multiple_of(b * 128, 128), 128)]
        fac[:, 128:256] = ident
        factor_slabs(fac)
        panel = dot(fac[:, 128:256], mat[b])
        mat[b] = panel

        def trail(i, c2):
            lhs = mat[b, :, pl.ds(pl.multiple_of(i * 128, 128), 128)]
            mat[i] = mat[i] - dot(lhs, mat[b], 0, 0)
            return c2
        lax.fori_loop(b + 1, 4, trail, 0)
        return carry
    lax.fori_loop(0, 4, block, 0)

    wide = mat[...].reshape(512, 1024)
    winv = wide[:, 512:1024]
    tri = lax.broadcasted_iota(jnp.int32, (NB, NB), 0) >= lax.broadcasted_iota(jnp.int32, (NB, NB), 1)
    for h in range(2):
        own = slice(256 * h, 256 * h + 256)
        gl[512:768, own] = jnp.where(tri, wide[own, own].T, 0.0)
    send(2)
    panel_wait()
    solved = dot(winv[:, 0:256], pc[0], 1, 1) + dot(winv[:, 256:512], pc[1], 1, 1)
    for h in range(2):
        rows = slice(256 * h, 256 * h + 256)
        gl[rows, :] = dot(winv[:, rows], solved, 0, 0)
        for q in range(2):
            @pl.when(col == q)
            def _():
                gl[rows, 0:256] = -winv[256 * q : 256 * q + 256, rows].T
        send(h)


def update_kernel(a, rr, gl, out, hi, lo):
    row = lax.axis_index("row")
    col = lax.axis_index("col")
    slot = pl.program_id(0)

    @pl.when(slot == 0)
    def _():
        g = gl[0:512, :]
        top = g.astype(jnp.bfloat16)
        hi[...] = top
        lo[...] = (g - top.astype(F32)).astype(jnp.bfloat16)

    def mul(p, q):
        return jnp.dot(p, q, preferred_element_type=F32)

    acc = jnp.zeros((NB, 512), F32)
    for kk in range(2):
        r = rr[slot % 4, kk, pl.ds(pl.multiple_of(slot // 4 * NB, NB), NB), :]
        top = r.astype(jnp.bfloat16)
        rest = (r - top.astype(F32)).astype(jnp.bfloat16)
        rows = slice(kk * NB, kk * NB + NB)
        acc = acc + mul(top, hi[rows, :]) + (mul(top, lo[rows, :]) + mul(rest, hi[rows, :]))
    panel = (lax.broadcasted_iota(jnp.int32, (NB, 512), 1) < NB) & (col < 2)
    out[...] = jnp.where(panel, 0.0, a[...]) - acc

    @pl.when((slot == 0) & (row < 2))
    def _():
        out[:, 256:512] = jnp.zeros((NB, NB), F32)
        for q in range(2):
            @pl.when((row == q) & (col == q))
            def _():
                out[:, 0:256] = gl[512:768, 256 * q : 256 * q + 256]

        @pl.when((col > 1) | ((row == 0) & (col == 1)))
        def _():
            out[:, 0:256] = jnp.zeros((NB, NB), F32)


def update(kernel, rr, gl):
    vmem = pl.BlockSpec(memory_space=pltpu.VMEM)
    return pl.pallas_call(
        update_kernel,
        out_shape=jax.ShapeDtypeStruct(kernel.shape, F32),
        grid=(8,),
        in_specs=[pl.BlockSpec((NB, 512), lambda j: (j, 0)), vmem, vmem],
        out_specs=pl.BlockSpec((NB, 512), lambda j: (j, 0)),
        scratch_shapes=[pltpu.VMEM((512, 512), jnp.bfloat16)] * 2,
        compiler_params=pltpu.CompilerParams(vmem_limit_bytes=24 << 20),
        name="update_trailing",
    )(kernel, rr, gl)


def local(kernel):
    rr, gl = gather_and_factor(kernel)
    return update(kernel, rr, gl)


def solution(mesh):
    placed = (P("row", "col"),)
    return jax.shard_map(
        local, mesh=mesh, in_specs=placed, out_specs=P("row", "col"), check_vma=False
    )
```

```python
import jax
import jax.numpy as jnp
from jax import lax
from jax.experimental import pallas as pl
from jax.experimental.pallas import tpu as pltpu
from jax.sharding import PartitionSpec as P

NB = 256
F32 = jnp.float32
MESH = pl.DeviceIdType.MESH
HI = lax.Precision.HIGHEST

SLAB = 16
CH = 64
DH = 32
PC_N = 512 // CH
D_N = NB // DH
LAGS = (0, 1, 2, 3)
ZP, ZM, YP, YM, XP, XM, PA, CP, CM, CF = range(10)


def dot(a, b, ca=1, cb=0):
    return lax.dot_general(
        a, b, (((ca,), (cb,)), ((), ())), precision=HI, preferred_element_type=F32
    )


def main_kernel(
    a, rr, gl, own_a, pc, oth, dd, headt, mat, fac,
    dsend, drecv, psend, precv, ppass, zsend, zrecv, ysend, yrecv,
    osend, orecv, gsend, grecv, lsem,
):
    row = lax.axis_index("row")
    col = lax.axis_index("col")
    x, k = row // 2, row % 2
    y, z = col // 8, col % 8

    def at(nx, ny, nz, nk):
        return ((nx % 4) * 2 + nk, (ny % 4) * 8 + nz % 8)

    near = {
        ZP: at(x, y, z + 1, k),
        ZM: at(x, y, z + 7, k),
        YP: at(x, y + 1, z, k),
        YM: at(x, y + 3, z, k),
        XP: at(x + 1, y, z, k),
        XM: at(x + 3, y, z, k),
        PA: at(x, y, z, 1 - k),
        CP: at(x + 1, y, z, 1),
        CM: at(x + 3, y, z, 1),
        CF: at(x + 2, y, z, 1),
    }
    barrier = pltpu.get_barrier_semaphore()
    for target in [near[way] for way in range(7)] + [
        at(x + 1, y, z, 1 - k), at(x + 3, y, z, 1 - k), at(x + 2, y, z, 0), at(x + 2, y, z, 1)
    ]:
        pl.semaphore_signal(barrier, inc=1, device_id=target, device_id_type=MESH)

    def remote(src, dst, send, recv, way):
        return pltpu.make_async_remote_copy(
            src_ref=src, dst_ref=dst, send_sem=send, recv_sem=recv,
            device_id=near[way], device_id_type=MESH,
        )

    top = pltpu.make_async_copy(a.at[pl.ds(0, NB), :], own_a.at[pl.ds(0, NB), :], lsem.at[0])
    top.start()
    low_rows = pl.ds(NB, 2048 - NB)
    bottom = pltpu.make_async_copy(a.at[low_rows, :], own_a.at[low_rows, :], lsem.at[4])
    bottom.start()
    top.wait()

    def rows_of(t, size):
        return pl.ds(pl.multiple_of(t * size, size), size)

    @pl.when(x == 0)
    def _():
        headt[...] = own_a[0:NB, :].T

    @pl.when((x == 0) & (y == 0) & (z < 2) & ((k == 0) | (z == 1)))
    def _():
        own = pltpu.make_async_copy(
            own_a.at[pl.ds(0, NB), pl.ds(0, NB)], dd.at[z + k], lsem.at[1]
        )
        own.start()
        own.wait()

    below, above, across = (y + 3) % 4, (y + 1) % 4, (y + 2) % 4

    def loop(n, body, first=0):
        def step(t, carry):
            body(t)
            return carry
        lax.fori_loop(first, n, step, 0)

    d_root, d_ways = [], []
    for i in range(3):
        dz = (z + 8 - min(i, 1)) % 8
        line = (x == 0) & (y == 0)
        root = line & (dz == 0)
        d_root.append(root)
        d_ways.append((
            (ZP, line & (dz <= 3)),
            (ZM, line & ((dz == 0) | (dz >= 6))),
            (YP, (x == 0) & (y <= 1)),
            (YM, (x == 0) & (y == 0)),
            (XP, x <= 1),
            (XM, x == 0),
        ))

    def d_copy(i, t, way):
        part = dd.at[i, rows_of(t, DH), :]
        return remote(part, part, dsend.at[way, i], drecv.at[i, t], way)

    def d_whole(i, way):
        return remote(dd.at[i], dd.at[i], dsend.at[way, i], drecv.at[i, 0], way)

    def d_block(i, begin, end):
        def one(t):
            if i == 2:
                d_copy(i, t, PA).wait_recv()
            else:
                @pl.when(jnp.logical_not(d_root[i]))
                def _():
                    d_copy(i, t, PA).wait_recv()

            for way, goes in d_ways[i]:
                @pl.when(goes)
                def _():
                    d_copy(i, t, way).start()
        loop(end, one, begin)

    def p_copy(kk, t, way):
        part = pc.at[kk, rows_of(t, CH), :]
        return remote(part, part, psend.at[way - PA, kk], precv.at[kk, t], way)

    def p_pass(kk, t):
        part = pc.at[kk, rows_of(t, CH), :]
        return remote(part, part, psend.at[0, kk], ppass.at[kk], PA)

    def p_whole(kk, way):
        return remote(pc.at[kk], pc.at[kk], psend.at[way - PA, kk], ppass.at[kk], way)

    def p_first(kk, t, way):
        recv = ppass.at[kk] if (way == PA and kk == 1) else precv.at[kk, t]
        return remote(
            headt.at[rows_of(t, CH), :], pc.at[kk, rows_of(t, CH), :],
            psend.at[way - PA, kk], recv, way,
        )

    def fill_own(kk):
        return pltpu.make_async_copy(headt, pc.at[kk], lsem.at[2])

    def p_step(kk, t):
        p_copy(kk, t, PA).wait_recv()
        p_pass(kk, t).start()

    held = (oth, rr)
    source = [z == 2 * x + g for g in range(2)]
    z_ways = []
    for g in range(2):
        dz = (z + 8 - 2 * x - g) % 8
        z_ways.append(((ZP, dz <= 3), (ZM, (dz == 0) | (dz >= 6))))

    def r_part(buf, ny, kk, t):
        return buf.at[ny, kk, rows_of(t, CH), :]

    def z_copy(g, kk, t, way):
        part = r_part(held[g], y, kk, t)
        return remote(part, part, zsend.at[way, g], zrecv.at[g, kk, t], way)

    def y_copy(g, ny, kk, t, way, slot):
        part = r_part(held[g], ny, kk, t)
        return remote(
            part, part, ysend.at[way - YP, slot, g], yrecv.at[way - YP, slot, g, kk, t], way
        )

    def o_copy(ny, kk, t):
        return remote(
            r_part(oth, ny, kk, t), r_part(rr, ny, kk, t), osend.at[0], orecv.at[0], PA
        )

    def own_step(g, kk, t):
        part = pc.at[kk, rows_of(t, CH), :]
        pltpu.make_async_copy(part, r_part(held[g], y, kk, t), lsem.at[3]).start()
        dst = r_part(held[g], y, kk, t)
        for way in (ZP, ZM):
            remote(part, dst, zsend.at[way, g], zrecv.at[g, kk, t], way).start()
        for way in (YP, YM):
            remote(
                part, dst, ysend.at[way - YP, 0, g], yrecv.at[way - YP, 0, g, kk, t], way
            ).start()
        if g == 0:
            remote(part, r_part(rr, y, kk, t), osend.at[0], orecv.at[0], PA).start()

    def pass_step(g, kk, t):
        z_copy(g, kk, t, ZP).wait_recv()
        for way, goes in z_ways[g]:
            @pl.when(goes)
            def _():
                z_copy(g, kk, t, way).start()
        y_copy(g, y, kk, t, YP, 0).start()
        y_copy(g, y, kk, t, YM, 0).start()
        if g == 0:
            o_copy(y, kk, t).start()

    def ring_step(g, kk, t):
        y_copy(g, below, kk, t, YP, 0).wait_recv()
        y_copy(g, above, kk, t, YM, 0).wait_recv()
        if kk == 0:
            y_copy(g, below, kk, t, YP, 1).start()
        else:
            y_copy(g, above, kk, t, YM, 1).start()
        if g == 0:
            o_copy(below, kk, t).start()
            o_copy(above, kk, t).start()

    def last_step(g, kk, t):
        y_copy(g, across, kk, t, YM if kk else YP, 1).wait_recv()
        if g == 0:
            o_copy(across, kk, t).start()

    def g_copy(h):
        part = gl.at[pl.ds(256 * h, 256), :]
        return remote(part, part, gsend.at[h], grecv.at[h], PA)

    @pl.when(k == 1)
    def _carry():
        pl.semaphore_wait(barrier, 11)

        @pl.when(d_root[2])
        def _():
            loop(D_N, lambda t: d_copy(2, t, PA).start())

        @pl.when(x == 0)
        def _():
            fill_own(1).start()

            def first(t):
                for way in (CP, CM, CF, PA):
                    p_first(1, t, way).start()
            loop(PC_N, first)
            fill_own(1).wait()

        def stage0(t):
            early = source[0] | source[1]
            first = jnp.where(early, 0, PC_N // 2)

            @pl.when((x > 0) & (t >= first) & (t < first + PC_N // 2))
            def _():
                for q in range(2):
                    for kk in range(2):
                        p_step(kk, 2 * (t - first) + q)

            @pl.when(x == 0)
            def _():
                p_copy(0, t, PA).wait_recv()
            for kk in range(2):
                for g in range(2):
                    @pl.when(source[g])
                    def _():
                        own_step(g, kk, t)

        def stage1(t):
            for kk in range(2):
                for g in range(2):
                    @pl.when(jnp.logical_not(source[g]))
                    def _():
                        pass_step(g, kk, t)

        def stage2(t):
            for kk in range(2):
                for g in range(2):
                    ring_step(g, kk, t)

        def stage3(t):
            for kk in range(2):
                for g in range(2):
                    last_step(g, kk, t)

        def body(t):
            for lag, stage in enumerate((stage0, stage1, stage2, stage3)):
                at_t = LAGS[lag]

                @pl.when((t >= at_t) & (t < PC_N + at_t))
                def _():
                    stage(t - at_t)
        loop(PC_N + LAGS[-1], body)

        for g in range(2):
            @pl.when(source[g])
            def _():
                pltpu.make_async_copy(pc, held[g].at[y], lsem.at[3]).wait()
        for g in range(2):
            for way, goes in z_ways[g]:
                @pl.when(goes)
                def _():
                    remote(rr.at[0], rr.at[0], zsend.at[way, g], orecv.at[0], way).wait_send()
            for way in (YP, YM):
                remote(rr.at[0], rr.at[0], ysend.at[way - YP, 0, g], orecv.at[0], way).wait_send()
                half = rr.at[0, 0]
                remote(half, half, ysend.at[way - YP, 1, g], orecv.at[0], way).wait_send()
        remote(oth, rr, osend.at[0], orecv.at[0], PA).wait_send()

        @pl.when(x == 0)
        def _():
            for way in (CP, CM, CF, PA):
                p_whole(1, way).wait_send()

        @pl.when(x > 0)
        def _():
            for kk in range(2):
                p_whole(kk, PA).wait_send()

        @pl.when(d_root[2])
        def _():
            d_whole(2, PA).wait_send()
        for h in range(3):
            g_copy(h).wait_recv()

    @pl.when(k == 0)
    def _factor():
        ident = (
            lax.broadcasted_iota(jnp.int32, (128, 128), 0)
            == lax.broadcasted_iota(jnp.int32, (128, 128), 1)
        ).astype(F32)
        mat[...] = jnp.zeros_like(mat)
        for b in range(4):
            mat[b, :, 512 + 128 * b : 640 + 128 * b] = ident
        pl.semaphore_wait(barrier, 11)

        @pl.when(x == 0)
        def _():
            def first(t):
                for way in (PA, CP, CM, CF):
                    p_first(0, t, way).start()
            loop(PC_N, first)
            fill_own(0).start()
        d_block(0, 0, D_N // 2)

        def d_rest():
            d_block(0, D_N // 2, D_N)
            d_block(1, 0, D_N)
            d_block(2, 0, D_N)

        def panel_wait():
            @pl.when(x == 0)
            def _():
                fill_own(0).wait()

            @pl.when(x > 0)
            def _():
                p_whole(0, PA).wait_recv()
            p_whole(1, PA).wait_recv()

        factor(dd, pc, gl, mat, fac, col, d_rest, panel_wait, lambda h: g_copy(h).start())

        remote(oth, rr, osend.at[0], orecv.at[0], PA).wait_recv()
        for i in range(3):
            for way, goes in d_ways[i]:
                @pl.when(goes)
                def _():
                    d_whole(i, way).wait_send()

        @pl.when(x == 0)
        def _():
            for way in (PA, CP, CM, CF):
                p_whole(0, way).wait_send()
        for h in range(3):
            g_copy(h).wait_send()

    bottom.wait()


def gather_and_factor(kernel):
    vmem = pl.BlockSpec(memory_space=pltpu.VMEM)
    dma = pltpu.SemaphoreType.DMA
    return pl.pallas_call(
        main_kernel,
        out_shape=(
            jax.ShapeDtypeStruct((4, 2, 512, NB), F32),
            jax.ShapeDtypeStruct((768, 512), F32),
            jax.ShapeDtypeStruct((2048, 512), F32),
        ),
        in_specs=[pl.BlockSpec(memory_space=pltpu.HBM)],
        out_specs=(vmem, vmem, vmem),
        scratch_shapes=[
            pltpu.VMEM((2, 512, NB), F32),
            pltpu.VMEM((4, 2, 512, NB), F32),
            pltpu.VMEM((3, NB, NB), F32),
            pltpu.VMEM((512, NB), F32),
            pltpu.VMEM((4, 128, 1024), F32),
            pltpu.VMEM((128, 256), F32),
            dma((7, 3)),
            dma((3, D_N)),
            dma((4, 2)),
            dma((2, PC_N)),
            dma((2,)),
            dma((2, 2)),
            dma((2, 2, PC_N)),
            dma((2, 2, 2)),
            dma((2, 2, 2, 2, PC_N)),
            dma((1,)),
            dma((1,)),
            dma((3,)),
            dma((3,)),
            dma((5,)),
        ],
        compiler_params=pltpu.CompilerParams(
            collective_id=0, has_side_effects=True, vmem_limit_bytes=44 << 20
        ),
        name="gather_and_factor",
    )(kernel)


def factor_slabs(fac):
    rows = lax.broadcasted_iota(jnp.int32, (8, 128), 0)

    def spread(tile, r):
        return jnp.broadcast_to(tile[r : r + 1, :], (8, 128))

    for i in range(128 // SLAB):
        lo = SLAB * i
        tiles = range(SLAB // 8)
        left = [fac[lo + 8 * t : lo + 8 * t + 8, 0:128] for t in tiles]
        right = [fac[lo + 8 * t : lo + 8 * t + 8, 128:256] for t in tiles]
        cols = [
            [jnp.broadcast_to(left[t][:, lo + q : lo + q + 1], (8, 128)) for t in tiles]
            for q in range(SLAB)
        ]
        for q in range(SLAB):
            tq, rq = q // 8, q % 8
            inv = lax.rsqrt(spread(cols[q][tq], rq))
            u_left = spread(left[tq], rq) * inv
            u_right = spread(right[tq], rq) * inv
            heads = {m: spread(cols[m][tq], rq) * inv for m in range(q + 1, SLAB)}
            for t in range(tq, SLAB // 8):
                coef = cols[q][t] * inv
                if t == tq:
                    coef = jnp.where(rows > rq, coef, 0.0)
                    scale = jnp.where(rows == rq, inv, 1.0)
                    left[t] = left[t] * scale
                    right[t] = right[t] * scale
                left[t] = left[t] - coef * u_left
                right[t] = right[t] - coef * u_right
                for m, head in heads.items():
                    cols[m][t] = cols[m][t] - coef * head
        for t in tiles:
            fac[lo + 8 * t : lo + 8 * t + 8, 0:128] = left[t]
            fac[lo + 8 * t : lo + 8 * t + 8, 128:256] = right[t]
        low = lo + SLAB
        if low < 128:
            upper = jnp.concatenate(left, axis=0)
            wide = jnp.concatenate([upper, jnp.concatenate(right, axis=0)], axis=1)
            end = min(low + SLAB, 128)
            fac[low:end, :] = fac[low:end, :] - dot(upper[:, low:end], wide, 0, 0)
            if end < 128:
                fac[end:128, :] = fac[end:128, :] - dot(upper[:, end:128], wide, 0, 0)


def split(v):
    top = v.astype(jnp.bfloat16)
    return top, (v - top.astype(F32)).astype(jnp.bfloat16)


def dot3(p, q, ca, cb):
    def one(u, v):
        return lax.dot_general(u, v, (((ca,), (cb,)), ((), ())), preferred_element_type=F32)
    return one(p[0], q[0]) + (one(p[0], q[1]) + one(p[1], q[0]))


def factor(dd, pc, gl, mat, fac, col, d_rest, panel_wait, send):
    ident = (
        lax.broadcasted_iota(jnp.int32, (128, 128), 0)
        == lax.broadcasted_iota(jnp.int32, (128, 128), 1)
    ).astype(F32)
    mat[0, :, 0:256] = dd[0, 0:128, :]

    def block(b, carry):
        here = pl.ds(pl.multiple_of(b * 128, 128), 128)
        window = pl.ds(pl.multiple_of(b * 128 + 128, 128), 512)
        fac[:, 0:128] = mat[b, :, here]
        fac[:, 128:256] = ident
        factor_slabs(fac)
        mat[b, :, here] = fac[:, 0:128]

        @pl.when(b == 0)
        def _():
            d_rest()
            mat[1, :, 0:256] = dd[0, 128:256, :]
            for q in range(2):
                mat[q, :, 256:512] = dd[1, 128 * q : 128 * q + 128, :]
                mat[q + 2, :, 256:512] = dd[2, 128 * q : 128 * q + 128, :]
        panel = dot(fac[:, 128:256], mat[b, :, window])
        mat[b, :, window] = panel

        def trail(i, c2):
            lhs = mat[b, :, pl.ds(pl.multiple_of(i * 128, 128), 128)]
            mat[i, :, window] = mat[i, :, window] - dot(lhs, mat[b, :, window], 0, 0)
            return c2
        lax.fori_loop(b + 1, 4, trail, 0)
        return carry
    lax.fori_loop(0, 4, block, 0)

    def winv(p, q):
        return mat[2 * p : 2 * p + 2, :, 512 + 256 * q : 768 + 256 * q].reshape(NB, NB)

    panel_wait()
    w = {pq: split(winv(*pq)) for pq in ((0, 0), (1, 0), (1, 1))}
    cols = [split(pc[q]) for q in range(2)]
    one = split(dot3(w[0, 0], cols[0], 1, 1))
    two = split(dot3(w[1, 0], cols[0], 1, 1) + dot3(w[1, 1], cols[1], 1, 1))

    def own(h, q):
        @pl.when(col == q)
        def _():
            gl[256 * h : 256 * h + 256, 0:256] = -winv(q, h).T

    gl[256:512, :] = dot3(w[1, 1], two, 0, 0)
    own(1, 0)
    own(1, 1)
    send(1)
    gl[0:256, :] = dot3(w[0, 0], one, 0, 0) + dot3(w[1, 0], two, 0, 0)
    own(0, 0)
    own(0, 1)
    send(0)
    tri = lax.broadcasted_iota(jnp.int32, (NB, NB), 0) >= lax.broadcasted_iota(jnp.int32, (NB, NB), 1)

    @pl.when(col < 2)
    def _():
        for h in range(2):
            span = slice(256 * h, 256 * h + 256)
            upper = mat[2 * h : 2 * h + 2, :, span].reshape(NB, NB)
            gl[512:768, span] = jnp.where(tri, upper.T, 0.0)
    send(2)


def update_kernel(a, rr, gl, out, hi, lo):
    row = lax.axis_index("row")
    col = lax.axis_index("col")
    slot = pl.program_id(0)

    @pl.when(slot == 0)
    def _():
        g = gl[0:512, :]
        top = g.astype(jnp.bfloat16)
        hi[...] = top
        lo[...] = (g - top.astype(F32)).astype(jnp.bfloat16)

    def mul(p, q):
        return jnp.dot(p, q, preferred_element_type=F32)

    acc = jnp.zeros((NB, 512), F32)
    for kk in range(2):
        r = rr[slot % 4, kk, pl.ds(pl.multiple_of(slot // 4 * NB, NB), NB), :]
        top = r.astype(jnp.bfloat16)
        rest = (r - top.astype(F32)).astype(jnp.bfloat16)
        rows = slice(kk * NB, kk * NB + NB)
        acc = acc + mul(top, hi[rows, :]) + (mul(top, lo[rows, :]) + mul(rest, hi[rows, :]))
    panel = (lax.broadcasted_iota(jnp.int32, (NB, 512), 1) < NB) & (col < 2)
    mine = a[pl.ds(pl.multiple_of(slot * NB, NB), NB), :]
    out[...] = jnp.where(panel, 0.0, mine) - acc

    @pl.when((slot == 0) & (row < 2))
    def _():
        out[:, 256:512] = jnp.zeros((NB, NB), F32)
        for q in range(2):
            @pl.when((row == q) & (col == q))
            def _():
                out[:, 0:256] = gl[512:768, 256 * q : 256 * q + 256]

        @pl.when((col > 1) | ((row == 0) & (col == 1)))
        def _():
            out[:, 0:256] = jnp.zeros((NB, NB), F32)


def update(kernel, rr, gl):
    vmem = pl.BlockSpec(memory_space=pltpu.VMEM)
    return pl.pallas_call(
        update_kernel,
        out_shape=jax.ShapeDtypeStruct(kernel.shape, F32),
        grid=(8,),
        in_specs=[vmem, vmem, vmem],
        out_specs=pl.BlockSpec((NB, 512), lambda j: (j, 0)),
        scratch_shapes=[pltpu.VMEM((512, 512), jnp.bfloat16)] * 2,
        compiler_params=pltpu.CompilerParams(vmem_limit_bytes=24 << 20),
        name="update_trailing",
    )(kernel, rr, gl)


def local(kernel):
    rr, gl, own = gather_and_factor(kernel)
    return update(own, rr, gl)


def solution(mesh):
    placed = (P("row", "col"),)
    return jax.shard_map(
        local, mesh=mesh, in_specs=placed, out_specs=P("row", "col"), check_vma=False
    )
```

```python
import jax
import jax.numpy as jnp
from jax import lax
from jax.experimental import pallas as pl
from jax.experimental.pallas import tpu as pltpu
from jax.sharding import PartitionSpec as P

NB = 256
F32 = jnp.float32
MESH = pl.DeviceIdType.MESH
HI = lax.Precision.HIGHEST

SLAB = 16
CH = 64
DH = 32
PC_N = 512 // CH
D_N = NB // DH
LAGS = (0, 1, 2, 3)
ZP, ZM, YP, YM, Z2, Z6, Y2, PA, CP, CM, CF = range(11)


def dot(a, b, ca=1, cb=0):
    return lax.dot_general(
        a, b, (((ca,), (cb,)), ((), ())), precision=HI, preferred_element_type=F32
    )


def main_kernel(
    a, rr, gl, own_a, pc, oth, dd, headt, wb, ub, fac,
    dsend, drecv, psend, precv, ppass, zsend, zrecv, ysend, yrecv,
    osend, orecv, gsend, grecv, lsem,
):
    row = lax.axis_index("row")
    col = lax.axis_index("col")
    x, k = row // 2, row % 2
    y, z = col // 8, col % 8

    def at(nx, ny, nz, nk):
        return ((nx % 4) * 2 + nk, (ny % 4) * 8 + nz % 8)

    urgent = jnp.where(z < 2, 1, z // 2)
    near = {
        ZP: at(x, y, z + 1, k),
        ZM: at(x, y, z + 7, k),
        YP: at(x, y + 1, z, k),
        YM: at(x, y + 3, z, k),
        Z2: at(x, y, z + 2, k),
        Z6: at(x, y, z + 6, k),
        Y2: at(x, y + 2, z, k),
        PA: at(x, y, z, 1 - k),
        CP: at(urgent, y, z, 1),
        CM: at(jnp.where(urgent == 1, 2, 1), y, z, 1),
        CF: at(jnp.where(urgent == 3, 2, 3), y, z, 1),
    }
    barrier = pltpu.get_barrier_semaphore()
    greeted = [near[way] for way in (ZP, ZM, YP, YM, Z2, Z6, Y2, PA)]
    greeted += [at(x + q, y, z, kk) for q in (1, 2, 3) for kk in (0, 1)]
    for target in greeted:
        pl.semaphore_signal(barrier, inc=1, device_id=target, device_id_type=MESH)

    def remote(src, dst, send, recv, way):
        return pltpu.make_async_remote_copy(
            src_ref=src, dst_ref=dst, send_sem=send, recv_sem=recv,
            device_id=near[way], device_id_type=MESH,
        )

    top = pltpu.make_async_copy(a.at[pl.ds(0, NB), :], own_a.at[pl.ds(0, NB), :], lsem.at[0])
    top.start()
    low_rows = pl.ds(NB, 2048 - NB)
    bottom = pltpu.make_async_copy(a.at[low_rows, :], own_a.at[low_rows, :], lsem.at[4])
    bottom.start()
    top.wait()

    def rows_of(t, size):
        return pl.ds(pl.multiple_of(t * size, size), size)

    @pl.when(x == 0)
    def _():
        headt[...] = own_a[0:NB, :].T

    @pl.when((x == 0) & (y == 0) & (z == 0) & (k == 0))
    def _():
        own = pltpu.make_async_copy(
            own_a.at[pl.ds(0, NB), pl.ds(0, NB)], dd.at[0], lsem.at[1]
        )
        own.start()
        own.wait()

    below, above, across = (y + 3) % 4, (y + 1) % 4, (y + 2) % 4

    def loop(n, body, first=0):
        def step(t, carry):
            body(t)
            return carry
        lax.fori_loop(first, n, step, 0)

    d_root, d_ways = [], []
    for i in range(3):
        dz = (z + 8 - i // 2) % 8
        d_root.append((y == 0) & (dz == 0))
        if i == 0:
            round_y = ((YP, d_root[i]), (YM, d_root[i]), (Y2, d_root[i]))
            along_z = (
                (Z2, (dz == 0) | (dz == 2)),
                (Z6, dz == 0),
                (ZP, (dz == 0) | (dz == 2)),
                (ZM, (dz == 0) | (dz == 6)),
            )
        else:
            round_y = ((YP, d_root[i]), (YM, ((y == 0) | (y == 3)) & (dz == 0)))
            along_z = ((ZP, dz <= 3), (ZM, (dz == 0) | (dz >= 6)))
        d_ways.append(round_y + along_z)

    def d_copy(i, t, way):
        part = dd.at[i, rows_of(t, DH), :]
        return remote(part, part, dsend.at[way, i], drecv.at[i, t], way)

    def d_whole(i, way):
        return remote(dd.at[i], dd.at[i], dsend.at[way, i], drecv.at[i, 0], way)

    def d_seed(i, kk, t):
        return remote(
            pc.at[kk, rows_of(t, DH), :], dd.at[i, rows_of(t, DH), :],
            dsend.at[PA, i], drecv.at[i, t], PA,
        )

    def d_block(i, begin, end):
        def one(t):
            if i == 0:
                @pl.when(jnp.logical_not(d_root[0] & (x == 0)))
                def _():
                    d_copy(i, t, PA).wait_recv()
            else:
                d_copy(i, t, PA).wait_recv()

            for way, goes in d_ways[i]:
                @pl.when(goes)
                def _():
                    d_copy(i, t, way).start()
        loop(end, one, begin)

    def p_copy(kk, t, way):
        part = pc.at[kk, rows_of(t, CH), :]
        return remote(part, part, psend.at[way - PA, kk], precv.at[kk, t], way)

    def p_pass(kk, t):
        part = pc.at[kk, rows_of(t, CH), :]
        return remote(part, part, psend.at[0, kk], ppass.at[kk], PA)

    def p_whole(kk, way):
        return remote(pc.at[kk], pc.at[kk], psend.at[way - PA, kk], ppass.at[kk], way)

    def p_first(kk, t, way):
        recv = ppass.at[kk] if (way == PA and kk == 1) else precv.at[kk, t]
        return remote(
            headt.at[rows_of(t, CH), :], pc.at[kk, rows_of(t, CH), :],
            psend.at[way - PA, kk], recv, way,
        )

    def send_first(kk):
        @pl.when(z < 2)
        def _():
            def every(t):
                for way in (CP, CM, CF, PA):
                    p_first(kk, t, way).start()
            loop(PC_N, every)

        @pl.when(z >= 2)
        def _():
            def one(t):
                for way in (CP, PA):
                    p_first(kk, t, way).start()
            loop(PC_N, one)

            def two(t):
                for way in (CM, CF):
                    p_first(kk, t, way).start()
            loop(PC_N, two)

    def fill_own(kk):
        return pltpu.make_async_copy(headt, pc.at[kk], lsem.at[2])

    def p_step(kk, t):
        p_copy(kk, t, PA).wait_recv()
        for i in ((0,), (1, 2))[kk]:
            @pl.when(d_root[i] & (t < NB // CH))
            def _():
                for q in range(CH // DH):
                    d_seed(i, kk, CH // DH * t + q).start()
        p_pass(kk, t).start()

    held = (oth, rr)
    source = [z == 2 * x + g for g in range(2)]
    z_ways = []
    for g in range(2):
        dz = (z + 8 - 2 * x - g) % 8
        z_ways.append(((ZP, dz <= 3), (ZM, (dz == 0) | (dz >= 6))))

    def r_part(buf, ny, kk, t):
        return buf.at[ny, kk, rows_of(t, CH), :]

    def z_copy(g, kk, t, way):
        part = r_part(held[g], y, kk, t)
        return remote(part, part, zsend.at[way, g], zrecv.at[g, kk, t], way)

    def y_copy(g, ny, kk, t, way, slot):
        part = r_part(held[g], ny, kk, t)
        return remote(
            part, part, ysend.at[way - YP, slot, g], yrecv.at[way - YP, slot, g, kk, t], way
        )

    def o_copy(ny, kk, t):
        return remote(
            r_part(oth, ny, kk, t), r_part(rr, ny, kk, t), osend.at[0], orecv.at[0], PA
        )

    def own_step(g, kk, t):
        part = pc.at[kk, rows_of(t, CH), :]
        pltpu.make_async_copy(part, r_part(held[g], y, kk, t), lsem.at[3]).start()
        dst = r_part(held[g], y, kk, t)
        for way in (ZP, ZM):
            remote(part, dst, zsend.at[way, g], zrecv.at[g, kk, t], way).start()
        for way in (YP, YM):
            remote(
                part, dst, ysend.at[way - YP, 0, g], yrecv.at[way - YP, 0, g, kk, t], way
            ).start()
        if g == 0:
            remote(part, r_part(rr, y, kk, t), osend.at[0], orecv.at[0], PA).start()

    def pass_step(g, kk, t):
        z_copy(g, kk, t, ZP).wait_recv()
        for way, goes in z_ways[g]:
            @pl.when(goes)
            def _():
                z_copy(g, kk, t, way).start()
        y_copy(g, y, kk, t, YP, 0).start()
        y_copy(g, y, kk, t, YM, 0).start()
        if g == 0:
            o_copy(y, kk, t).start()

    def ring_step(g, kk, t):
        y_copy(g, below, kk, t, YP, 0).wait_recv()
        y_copy(g, above, kk, t, YM, 0).wait_recv()
        if kk == 0:
            y_copy(g, below, kk, t, YP, 1).start()
        else:
            y_copy(g, above, kk, t, YM, 1).start()
        if g == 0:
            o_copy(below, kk, t).start()
            o_copy(above, kk, t).start()

    def last_step(g, kk, t):
        y_copy(g, across, kk, t, YM if kk else YP, 1).wait_recv()
        if g == 0:
            o_copy(across, kk, t).start()

    def g_copy(h):
        part = gl.at[pl.ds(256 * h, 256), :]
        return remote(part, part, gsend.at[h], grecv.at[h], PA)

    @pl.when(k == 1)
    def _carry():
        pl.semaphore_wait(barrier, 14)

        @pl.when(x == 0)
        def _():
            send_first(1)
            fill_own(1).start()
            fill_own(1).wait()
            for i in (1, 2):
                @pl.when(d_root[i])
                def _():
                    loop(D_N, lambda t: d_seed(i, 1, t).start())

        def stage0(t):
            early = source[0] | source[1] | d_root[0] | d_root[2]
            first = jnp.where(early, 0, PC_N // 2)

            @pl.when((x > 0) & (t >= first) & (t < first + PC_N // 2))
            def _():
                for q in range(2):
                    for kk in range(2):
                        p_step(kk, 2 * (t - first) + q)

            @pl.when(x == 0)
            def _():
                p_copy(0, t, PA).wait_recv()
            for kk in range(2):
                for g in range(2):
                    @pl.when(source[g])
                    def _():
                        own_step(g, kk, t)

        def stage1(t):
            for kk in range(2):
                for g in range(2):
                    @pl.when(jnp.logical_not(source[g]))
                    def _():
                        pass_step(g, kk, t)

        def stage2(t):
            for kk in range(2):
                for g in range(2):
                    ring_step(g, kk, t)

        def stage3(t):
            for kk in range(2):
                for g in range(2):
                    last_step(g, kk, t)

        def body(t):
            for lag, stage in enumerate((stage0, stage1, stage2, stage3)):
                at_t = LAGS[lag]

                @pl.when((t >= at_t) & (t < PC_N + at_t))
                def _():
                    stage(t - at_t)
        loop(PC_N + LAGS[-1], body)

        for g in range(2):
            @pl.when(source[g])
            def _():
                pltpu.make_async_copy(pc, held[g].at[y], lsem.at[3]).wait()
        for g in range(2):
            for way, goes in z_ways[g]:
                @pl.when(goes)
                def _():
                    remote(rr.at[0], rr.at[0], zsend.at[way, g], orecv.at[0], way).wait_send()
            for way in (YP, YM):
                remote(rr.at[0], rr.at[0], ysend.at[way - YP, 0, g], orecv.at[0], way).wait_send()
                half = rr.at[0, 0]
                remote(half, half, ysend.at[way - YP, 1, g], orecv.at[0], way).wait_send()
        remote(oth, rr, osend.at[0], orecv.at[0], PA).wait_send()

        @pl.when(x == 0)
        def _():
            for way in (CP, CM, CF, PA):
                p_whole(1, way).wait_send()

        @pl.when(x > 0)
        def _():
            for kk in range(2):
                p_whole(kk, PA).wait_send()

        for i in range(3):
            seeds = d_root[i] & (x > 0) if i == 0 else d_root[i]

            @pl.when(seeds)
            def _():
                d_whole(i, PA).wait_send()
        for h in range(3):
            g_copy(h).wait_recv()

    @pl.when(k == 0)
    def _factor():
        pl.semaphore_wait(barrier, 14)

        @pl.when(x == 0)
        def _():
            send_first(0)
            fill_own(0).start()
        d_block(0, 0, D_N // 2)

        def d_more(b, j):
            q = D_N // 4
            if b == 0:
                if j < 2:
                    d_block(0, (2 + j) * q, (3 + j) * q)
                else:
                    d_block(1, (j - 2) * 2 * q, (j - 1) * 2 * q)
            else:
                d_block(2, j * q, (j + 1) * q)

        def panel_wait():
            @pl.when(x == 0)
            def _():
                fill_own(0).wait()

            @pl.when(x > 0)
            def _():
                p_whole(0, PA).wait_recv()
            p_whole(1, PA).wait_recv()

        factor(dd, pc, gl, wb, ub, fac, col, d_more, panel_wait, lambda h: g_copy(h).start())

        remote(oth, rr, osend.at[0], orecv.at[0], PA).wait_recv()
        for i in range(3):
            for way, goes in d_ways[i]:
                @pl.when(goes)
                def _():
                    d_whole(i, way).wait_send()

        @pl.when(x == 0)
        def _():
            for way in (PA, CP, CM, CF):
                p_whole(0, way).wait_send()
        for h in range(3):
            g_copy(h).wait_send()

    bottom.wait()


def gather_and_factor(kernel):
    vmem = pl.BlockSpec(memory_space=pltpu.VMEM)
    dma = pltpu.SemaphoreType.DMA
    return pl.pallas_call(
        main_kernel,
        out_shape=(
            jax.ShapeDtypeStruct((4, 2, 512, NB), F32),
            jax.ShapeDtypeStruct((768, 512), F32),
            jax.ShapeDtypeStruct((2048, 512), F32),
        ),
        in_specs=[pl.BlockSpec(memory_space=pltpu.HBM)],
        out_specs=(vmem, vmem, vmem),
        scratch_shapes=[
            pltpu.VMEM((2, 512, NB), F32),
            pltpu.VMEM((4, 2, 512, NB), F32),
            pltpu.VMEM((3, NB, NB), F32),
            pltpu.VMEM((512, NB), F32),
            pltpu.VMEM((2, NB, NB), F32),
            pltpu.VMEM((2, NB, NB), F32),
            pltpu.VMEM((128, 256), F32),
            dma((8, 3)),
            dma((3, D_N)),
            dma((4, 2)),
            dma((2, PC_N)),
            dma((2,)),
            dma((2, 2)),
            dma((2, 2, PC_N)),
            dma((2, 2, 2)),
            dma((2, 2, 2, 2, PC_N)),
            dma((1,)),
            dma((1,)),
            dma((3,)),
            dma((3,)),
            dma((5,)),
        ],
        compiler_params=pltpu.CompilerParams(
            collective_id=0, has_side_effects=True, vmem_limit_bytes=44 << 20
        ),
        name="gather_and_factor",
    )(kernel)


def factor_slabs(fac, between):
    rows = lax.broadcasted_iota(jnp.int32, (8, 128), 0)

    def spread(tile, r):
        return jnp.broadcast_to(tile[r : r + 1, :], (8, 128))

    for i in range(128 // SLAB):
        lo = SLAB * i
        tiles = range(SLAB // 8)
        left = [fac[lo + 8 * t : lo + 8 * t + 8, 0:128] for t in tiles]
        right = [fac[lo + 8 * t : lo + 8 * t + 8, 128:256] for t in tiles]
        cols = [
            [jnp.broadcast_to(left[t][:, lo + q : lo + q + 1], (8, 128)) for t in tiles]
            for q in range(SLAB)
        ]
        for q in range(SLAB):
            tq, rq = q // 8, q % 8
            inv = lax.rsqrt(spread(cols[q][tq], rq))
            u_left = spread(left[tq], rq) * inv
            u_right = spread(right[tq], rq) * inv
            heads = {m: spread(cols[m][tq], rq) * inv for m in range(q + 1, SLAB)}
            for t in range(tq, SLAB // 8):
                coef = cols[q][t] * inv
                if t == tq:
                    coef = jnp.where(rows > rq, coef, 0.0)
                    scale = jnp.where(rows == rq, inv, 1.0)
                    left[t] = left[t] * scale
                    right[t] = right[t] * scale
                left[t] = left[t] - coef * u_left
                right[t] = right[t] - coef * u_right
                for m, head in heads.items():
                    cols[m][t] = cols[m][t] - coef * head
        for t in tiles:
            fac[lo + 8 * t : lo + 8 * t + 8, 0:128] = left[t]
            fac[lo + 8 * t : lo + 8 * t + 8, 128:256] = right[t]
        low = lo + SLAB
        if i % 2 == 1:
            between(i // 2)
        if low < 128:
            upper = jnp.concatenate(left, axis=0)
            wide = jnp.concatenate([upper, jnp.concatenate(right, axis=0)], axis=1)
            end = min(low + SLAB, 128)
            fac[low:end, :] = fac[low:end, :] - dot(upper[:, low:end], wide, 0, 0)
            if end < 128:
                fac[end:128, :] = fac[end:128, :] - dot(upper[:, end:128], wide, 0, 0)


def split(v):
    top = v.astype(jnp.bfloat16)
    return top, (v - top.astype(F32)).astype(jnp.bfloat16)


def dot3(p, q, ca, cb):
    def one(u, v):
        return lax.dot_general(u, v, (((ca,), (cb,)), ((), ())), preferred_element_type=F32)
    return one(p[0], q[0]) + (one(p[0], q[1]) + one(p[1], q[0]))


def factor(dd, pc, gl, wb, ub, fac, col, d_more, panel_wait, send):
    ident = (
        lax.broadcasted_iota(jnp.int32, (128, 128), 0)
        == lax.broadcasted_iota(jnp.int32, (128, 128), 1)
    ).astype(F32)

    def half(h, src, between, middle):
        lo, hi = slice(0, 128), slice(128, 256)
        fac[:, 0:128] = src[lo, lo]
        fac[:, 128:256] = ident
        factor_slabs(fac, lambda j: between(0, j))
        w0 = fac[:, 128:256]
        wb[h, lo, lo] = w0
        wb[h, lo, hi] = jnp.zeros((128, 128), F32)
        ub[h, lo, lo] = fac[:, 0:128]
        u01 = dot(w0, src[lo, hi])
        ub[h, lo, hi] = u01
        fac[:, 0:128] = src[hi, hi] - dot(u01, u01, 0, 0)
        fac[:, 128:256] = ident
        middle()
        factor_slabs(fac, lambda j: between(1, j))
        w1 = fac[:, 128:256]
        ub[h, hi, hi] = fac[:, 0:128]
        wb[h, hi, hi] = w1
        wb[h, hi, lo] = -dot(w1, dot(u01, w0, 0, 0))

    half(0, dd.at[0], d_more, lambda: None)
    w_one = wb[0]
    v = dot(w_one, dd[1])
    ub[1] = dd[2] - dot(v, v, 0, 0)
    w_one = split(w_one)
    v = split(v)
    kept = {}

    def middle():
        panel_wait()
        one = dot3(w_one, split(pc[0]), 1, 1)
        kept["one"] = dot3(w_one, split(one), 0, 0)
        kept["two"] = pc[1].T - dot3(v, split(one), 0, 0)
        kept["mix"] = split(dot3(w_one, v, 0, 0))

    half(1, ub.at[1], lambda b, j: None, middle)
    w_two = split(wb[1])
    two = dot3(w_two, split(kept["two"]), 1, 0)
    g_two = dot3(w_two, split(two), 0, 0)
    gl[256:512, :] = g_two

    @pl.when(col == 0)
    def _():
        gl[256:512, 0:256] = jnp.zeros((NB, NB), F32)

    @pl.when(col == 1)
    def _():
        gl[256:512, 0:256] = -wb[1].T
    send(1)
    gl[0:256, :] = kept["one"] - dot3(kept["mix"], split(g_two), 1, 0)

    @pl.when(col == 0)
    def _():
        gl[0:256, 0:256] = -wb[0].T

    @pl.when(col == 1)
    def _():
        gl[0:256, 0:256] = dot3(kept["mix"], w_two, 1, 1)
    send(0)
    tri = lax.broadcasted_iota(jnp.int32, (NB, NB), 0) >= lax.broadcasted_iota(jnp.int32, (NB, NB), 1)

    @pl.when(col < 2)
    def _():
        for h in range(2):
            gl[512:768, 256 * h : 256 * h + 256] = jnp.where(tri, ub[h].T, 0.0)
    send(2)


def update_kernel(a, rr, gl, out, hi, lo):
    row = lax.axis_index("row")
    col = lax.axis_index("col")
    slot = pl.program_id(0)

    @pl.when(slot == 0)
    def _():
        g = gl[0:512, :]
        top = g.astype(jnp.bfloat16)
        hi[...] = top
        lo[...] = (g - top.astype(F32)).astype(jnp.bfloat16)

    def mul(p, q):
        return jnp.dot(p, q, preferred_element_type=F32)

    acc = jnp.zeros((NB, 512), F32)
    for kk in range(2):
        r = rr[slot % 4, kk, pl.ds(pl.multiple_of(slot // 4 * NB, NB), NB), :]
        top = r.astype(jnp.bfloat16)
        rest = (r - top.astype(F32)).astype(jnp.bfloat16)
        rows = slice(kk * NB, kk * NB + NB)
        acc = acc + mul(top, hi[rows, :]) + (mul(top, lo[rows, :]) + mul(rest, hi[rows, :]))
    panel = (lax.broadcasted_iota(jnp.int32, (NB, 512), 1) < NB) & (col < 2)
    mine = a[pl.ds(pl.multiple_of(slot * NB, NB), NB), :]
    out[...] = jnp.where(panel, 0.0, mine) - acc

    @pl.when((slot == 0) & (row < 2))
    def _():
        out[:, 256:512] = jnp.zeros((NB, NB), F32)
        for q in range(2):
            @pl.when((row == q) & (col == q))
            def _():
                out[:, 0:256] = gl[512:768, 256 * q : 256 * q + 256]

        @pl.when((col > 1) | ((row == 0) & (col == 1)))
        def _():
            out[:, 0:256] = jnp.zeros((NB, NB), F32)


def update(kernel, rr, gl):
    vmem = pl.BlockSpec(memory_space=pltpu.VMEM)
    return pl.pallas_call(
        update_kernel,
        out_shape=jax.ShapeDtypeStruct(kernel.shape, F32),
        grid=(8,),
        in_specs=[vmem, vmem, vmem],
        out_specs=pl.BlockSpec((NB, 512), lambda j: (j, 0)),
        scratch_shapes=[pltpu.VMEM((512, 512), jnp.bfloat16)] * 2,
        compiler_params=pltpu.CompilerParams(vmem_limit_bytes=24 << 20),
        name="update_trailing",
    )(kernel, rr, gl)


def local(kernel):
    rr, gl, own = gather_and_factor(kernel)
    return update(own, rr, gl)


def solution(mesh):
    placed = (P("row", "col"),)
    return jax.shard_map(
        local, mesh=mesh, in_specs=placed, out_specs=P("row", "col"), check_vma=False
    )
```

```python
import jax
import jax.numpy as jnp
from jax import lax
from jax.experimental import pallas as pl
from jax.experimental.pallas import tpu as pltpu
from jax.sharding import PartitionSpec as P

NB = 256
F32 = jnp.float32
MESH = pl.DeviceIdType.MESH
HI = lax.Precision.HIGHEST

SLAB = 16
CH = 64
DH = 32
PC_N = 512 // CH
D_N = NB // DH
LAGS = (0, 1, 2, 3)
ZP, ZM, YP, YM, Z2, Z6, Y2, PA, CP, CM, CF = range(11)


def dot(a, b, ca=1, cb=0):
    return lax.dot_general(
        a, b, (((ca,), (cb,)), ((), ())), precision=HI, preferred_element_type=F32
    )


def main_kernel(
    a, rr, gl, own_a, pc, oth, dd, headt, wb, ub, fac,
    dsend, drecv, psend, precv, ppass, zsend, zrecv, ysend, yrecv,
    osend, orecv, gsend, grecv, lsem,
):
    row = lax.axis_index("row")
    col = lax.axis_index("col")
    x, k = row // 2, row % 2
    y, z = col // 8, col % 8

    def at(nx, ny, nz, nk):
        return ((nx % 4) * 2 + nk, (ny % 4) * 8 + nz % 8)

    urgent = jnp.where(z < 2, 1, z // 2)
    near = {
        ZP: at(x, y, z + 1, k),
        ZM: at(x, y, z + 7, k),
        YP: at(x, y + 1, z, k),
        YM: at(x, y + 3, z, k),
        Z2: at(x, y, z + 2, k),
        Z6: at(x, y, z + 6, k),
        Y2: at(x, y + 2, z, k),
        PA: at(x, y, z, 1 - k),
        CP: at(urgent, y, z, 1),
        CM: at(jnp.where(urgent == 1, 2, 1), y, z, 1),
        CF: at(jnp.where(urgent == 3, 2, 3), y, z, 1),
    }
    barrier = pltpu.get_barrier_semaphore()
    greeted = [near[way] for way in (ZP, ZM, YP, YM, Z2, Z6, Y2, PA)]
    greeted += [at(x + q, y, z, kk) for q in (1, 2, 3) for kk in (0, 1)]
    for target in greeted:
        pl.semaphore_signal(barrier, inc=1, device_id=target, device_id_type=MESH)

    def remote(src, dst, send, recv, way):
        return pltpu.make_async_remote_copy(
            src_ref=src, dst_ref=dst, send_sem=send, recv_sem=recv,
            device_id=near[way], device_id_type=MESH,
        )

    top = pltpu.make_async_copy(a.at[pl.ds(0, NB), :], own_a.at[pl.ds(0, NB), :], lsem.at[0])
    top.start()
    low_rows = pl.ds(NB, 2048 - NB)
    bottom = pltpu.make_async_copy(a.at[low_rows, :], own_a.at[low_rows, :], lsem.at[4])
    bottom.start()
    top.wait()

    def rows_of(t, size):
        return pl.ds(pl.multiple_of(t * size, size), size)

    @pl.when(x == 0)
    def _():
        headt[...] = own_a[0:NB, :].T

    @pl.when((x == 0) & (y == 0) & (z == 0) & (k == 0))
    def _():
        own = pltpu.make_async_copy(
            own_a.at[pl.ds(0, NB), pl.ds(0, NB)], dd.at[0], lsem.at[1]
        )
        own.start()
        own.wait()

    below, above, across = (y + 3) % 4, (y + 1) % 4, (y + 2) % 4

    def loop(n, body, first=0):
        def step(t, carry):
            body(t)
            return carry
        lax.fori_loop(first, n, step, 0)

    d_root, d_ways = [], []
    for i in range(3):
        dz = (z + 8 - i // 2) % 8
        d_root.append((y == 0) & (dz == 0))
        if i == 0:
            round_y = ((YP, d_root[i]), (YM, d_root[i]), (Y2, d_root[i]))
            along_z = ((ZP, dz <= 3), (ZM, (dz == 0) | (dz >= 6)))
        else:
            round_y = ((YP, d_root[i]), (YM, ((y == 0) | (y == 3)) & (dz == 0)))
            along_z = ((ZP, dz <= 3), (ZM, (dz == 0) | (dz >= 6)))
        d_ways.append(round_y + along_z)

    def d_copy(i, t, way):
        part = dd.at[i, rows_of(t, DH), :]
        return remote(part, part, dsend.at[way, i], drecv.at[i, t], way)

    def d_whole(i, way):
        return remote(dd.at[i], dd.at[i], dsend.at[way, i], drecv.at[i, 0], way)

    def d_seed(i, kk, t):
        return remote(
            pc.at[kk, rows_of(t, DH), :], dd.at[i, rows_of(t, DH), :],
            dsend.at[PA, i], drecv.at[i, t], PA,
        )

    def d_block(i, begin, end):
        def one(t):
            if i == 0:
                @pl.when(jnp.logical_not(d_root[0] & (x == 0)))
                def _():
                    d_copy(i, t, PA).wait_recv()
            else:
                d_copy(i, t, PA).wait_recv()

            for way, goes in d_ways[i]:
                @pl.when(goes)
                def _():
                    d_copy(i, t, way).start()
        loop(end, one, begin)

    def p_copy(kk, t, way):
        part = pc.at[kk, rows_of(t, CH), :]
        return remote(part, part, psend.at[way - PA, kk], precv.at[kk, t], way)

    def p_pass(kk, t):
        part = pc.at[kk, rows_of(t, CH), :]
        return remote(part, part, psend.at[0, kk], ppass.at[kk], PA)

    def p_whole(kk, way):
        return remote(pc.at[kk], pc.at[kk], psend.at[way - PA, kk], ppass.at[kk], way)

    def p_first(kk, t, way):
        recv = ppass.at[kk] if (way == PA and kk == 1) else precv.at[kk, t]
        return remote(
            headt.at[rows_of(t, CH), :], pc.at[kk, rows_of(t, CH), :],
            psend.at[way - PA, kk], recv, way,
        )

    def send_first(kk):
        @pl.when(z < 2)
        def _():
            def every(t):
                for way in (CP, CM, CF, PA):
                    p_first(kk, t, way).start()
            loop(PC_N, every)

        @pl.when(z >= 2)
        def _():
            def one(t):
                for way in (CP, PA):
                    p_first(kk, t, way).start()
            loop(PC_N, one)

            def two(t):
                for way in (CM, CF):
                    p_first(kk, t, way).start()
            loop(PC_N, two)

    def fill_own(kk):
        return pltpu.make_async_copy(headt, pc.at[kk], lsem.at[2])

    def p_step(kk, t):
        p_copy(kk, t, PA).wait_recv()
        for i in ((0,), (1, 2))[kk]:
            @pl.when(d_root[i] & (t < NB // CH))
            def _():
                for q in range(CH // DH):
                    d_seed(i, kk, CH // DH * t + q).start()
        p_pass(kk, t).start()

    held = (oth, rr)
    source = [z == 2 * x + g for g in range(2)]
    z_ways = []
    for g in range(2):
        dz = (z + 8 - 2 * x - g) % 8
        z_ways.append(((ZP, dz <= 3), (ZM, (dz == 0) | (dz >= 6))))

    def r_part(buf, ny, kk, t):
        return buf.at[ny, kk, rows_of(t, CH), :]

    def z_copy(g, kk, t, way):
        part = r_part(held[g], y, kk, t)
        return remote(part, part, zsend.at[way, g], zrecv.at[g, kk, t], way)

    def y_copy(g, ny, kk, t, way, slot):
        part = r_part(held[g], ny, kk, t)
        return remote(
            part, part, ysend.at[way - YP, slot, g], yrecv.at[way - YP, slot, g, kk, t], way
        )

    def o_copy(ny, kk, t):
        return remote(
            r_part(oth, ny, kk, t), r_part(rr, ny, kk, t), osend.at[0], orecv.at[0], PA
        )

    def own_step(g, kk, t):
        part = pc.at[kk, rows_of(t, CH), :]
        pltpu.make_async_copy(part, r_part(held[g], y, kk, t), lsem.at[3]).start()
        dst = r_part(held[g], y, kk, t)
        for way in (ZP, ZM):
            remote(part, dst, zsend.at[way, g], zrecv.at[g, kk, t], way).start()
        for way in (YP, YM):
            remote(
                part, dst, ysend.at[way - YP, 0, g], yrecv.at[way - YP, 0, g, kk, t], way
            ).start()
        if g == 0:
            remote(part, r_part(rr, y, kk, t), osend.at[0], orecv.at[0], PA).start()

    def pass_step(g, kk, t):
        z_copy(g, kk, t, ZP).wait_recv()
        for way, goes in z_ways[g]:
            @pl.when(goes)
            def _():
                z_copy(g, kk, t, way).start()
        y_copy(g, y, kk, t, YP, 0).start()
        y_copy(g, y, kk, t, YM, 0).start()
        if g == 0:
            o_copy(y, kk, t).start()

    def ring_step(g, kk, t):
        y_copy(g, below, kk, t, YP, 0).wait_recv()
        y_copy(g, above, kk, t, YM, 0).wait_recv()
        if kk == 0:
            y_copy(g, below, kk, t, YP, 1).start()
        else:
            y_copy(g, above, kk, t, YM, 1).start()
        if g == 0:
            o_copy(below, kk, t).start()
            o_copy(above, kk, t).start()

    def last_step(g, kk, t):
        y_copy(g, across, kk, t, YM if kk else YP, 1).wait_recv()
        if g == 0:
            o_copy(across, kk, t).start()

    def g_copy(h):
        part = gl.at[pl.ds(256 * h, 256), :]
        return remote(part, part, gsend.at[h], grecv.at[h], PA)

    @pl.when(k == 1)
    def _carry():
        pl.semaphore_wait(barrier, 14)

        @pl.when(x == 0)
        def _():
            send_first(1)
            fill_own(1).start()
            fill_own(1).wait()
            for i in (1, 2):
                @pl.when(d_root[i])
                def _():
                    loop(D_N, lambda t: d_seed(i, 1, t).start())

        def stage0(t):
            early = source[0] | source[1] | d_root[0] | d_root[2]
            first = jnp.where(early, 0, PC_N // 2)

            @pl.when((x > 0) & (t >= first) & (t < first + PC_N // 2))
            def _():
                for q in range(2):
                    for kk in range(2):
                        p_step(kk, 2 * (t - first) + q)

            @pl.when(x == 0)
            def _():
                p_copy(0, t, PA).wait_recv()
            for kk in range(2):
                for g in range(2):
                    @pl.when(source[g])
                    def _():
                        own_step(g, kk, t)

        def stage1(t):
            for kk in range(2):
                for g in range(2):
                    @pl.when(jnp.logical_not(source[g]))
                    def _():
                        pass_step(g, kk, t)

        def stage2(t):
            for kk in range(2):
                for g in range(2):
                    ring_step(g, kk, t)

        def stage3(t):
            for kk in range(2):
                for g in range(2):
                    last_step(g, kk, t)

        def body(t):
            for lag, stage in enumerate((stage0, stage1, stage2, stage3)):
                at_t = LAGS[lag]

                @pl.when((t >= at_t) & (t < PC_N + at_t))
                def _():
                    stage(t - at_t)
        loop(PC_N + LAGS[-1], body)

        for g in range(2):
            @pl.when(source[g])
            def _():
                pltpu.make_async_copy(pc, held[g].at[y], lsem.at[3]).wait()
        for g in range(2):
            for way, goes in z_ways[g]:
                @pl.when(goes)
                def _():
                    remote(rr.at[0], rr.at[0], zsend.at[way, g], orecv.at[0], way).wait_send()
            for way in (YP, YM):
                remote(rr.at[0], rr.at[0], ysend.at[way - YP, 0, g], orecv.at[0], way).wait_send()
                half = rr.at[0, 0]
                remote(half, half, ysend.at[way - YP, 1, g], orecv.at[0], way).wait_send()
        remote(oth, rr, osend.at[0], orecv.at[0], PA).wait_send()

        @pl.when(x == 0)
        def _():
            for way in (CP, CM, CF, PA):
                p_whole(1, way).wait_send()

        @pl.when(x > 0)
        def _():
            for kk in range(2):
                p_whole(kk, PA).wait_send()

        for i in range(3):
            seeds = d_root[i] & (x > 0) if i == 0 else d_root[i]

            @pl.when(seeds)
            def _():
                d_whole(i, PA).wait_send()
        for h in range(2):
            g_copy(h).wait_recv()

        @pl.when(col < 2)
        def _():
            g_copy(2).wait_recv()

    @pl.when(k == 0)
    def _factor():
        pl.semaphore_wait(barrier, 14)

        @pl.when(x == 0)
        def _():
            send_first(0)
            fill_own(0).start()
        d_block(0, 0, D_N // 2)

        def d_more(b, j):
            q = D_N // 4
            if b == 0:
                if j < 2:
                    d_block(0, (2 + j) * q, (3 + j) * q)
                else:
                    d_block(1, (j - 2) * 2 * q, (j - 1) * 2 * q)
            else:
                d_block(2, j * q, (j + 1) * q)

        def panel_wait():
            @pl.when(x == 0)
            def _():
                fill_own(0).wait()

            @pl.when(x > 0)
            def _():
                p_whole(0, PA).wait_recv()
            p_whole(1, PA).wait_recv()

        factor(dd, pc, gl, wb, ub, fac, col, d_more, panel_wait, lambda h: g_copy(h).start())

        remote(oth, rr, osend.at[0], orecv.at[0], PA).wait_recv()
        for i in range(3):
            for way, goes in d_ways[i]:
                @pl.when(goes)
                def _():
                    d_whole(i, way).wait_send()

        @pl.when(x == 0)
        def _():
            for way in (PA, CP, CM, CF):
                p_whole(0, way).wait_send()
        for h in range(2):
            g_copy(h).wait_send()

        @pl.when(col < 2)
        def _():
            g_copy(2).wait_send()

    bottom.wait()


def gather_and_factor(kernel):
    vmem = pl.BlockSpec(memory_space=pltpu.VMEM)
    dma = pltpu.SemaphoreType.DMA
    return pl.pallas_call(
        main_kernel,
        out_shape=(
            jax.ShapeDtypeStruct((4, 2, 512, NB), F32),
            jax.ShapeDtypeStruct((768, 512), F32),
            jax.ShapeDtypeStruct((2048, 512), F32),
        ),
        in_specs=[pl.BlockSpec(memory_space=pltpu.HBM)],
        out_specs=(vmem, vmem, vmem),
        scratch_shapes=[
            pltpu.VMEM((2, 512, NB), F32),
            pltpu.VMEM((4, 2, 512, NB), F32),
            pltpu.VMEM((3, NB, NB), F32),
            pltpu.VMEM((512, NB), F32),
            pltpu.VMEM((2, NB, NB), F32),
            pltpu.VMEM((2, NB, NB), F32),
            pltpu.VMEM((128, 256), F32),
            dma((8, 3)),
            dma((3, D_N)),
            dma((4, 2)),
            dma((2, PC_N)),
            dma((2,)),
            dma((2, 2)),
            dma((2, 2, PC_N)),
            dma((2, 2, 2)),
            dma((2, 2, 2, 2, PC_N)),
            dma((1,)),
            dma((1,)),
            dma((3,)),
            dma((3,)),
            dma((5,)),
        ],
        compiler_params=pltpu.CompilerParams(
            collective_id=0, has_side_effects=True, vmem_limit_bytes=44 << 20
        ),
        name="gather_and_factor",
    )(kernel)


def factor_slabs(fac, between):
    rows = lax.broadcasted_iota(jnp.int32, (8, 128), 0)

    def spread(tile, r):
        return jnp.broadcast_to(tile[r : r + 1, :], (8, 128))

    for i in range(128 // SLAB):
        lo = SLAB * i
        tiles = range(SLAB // 8)
        left = [fac[lo + 8 * t : lo + 8 * t + 8, 0:128] for t in tiles]
        right = [fac[lo + 8 * t : lo + 8 * t + 8, 128:256] for t in tiles]
        cols = [
            [jnp.broadcast_to(left[t][:, lo + q : lo + q + 1], (8, 128)) for t in tiles]
            for q in range(SLAB)
        ]
        for q in range(SLAB):
            tq, rq = q // 8, q % 8
            inv = lax.rsqrt(spread(cols[q][tq], rq))
            u_left = spread(left[tq], rq) * inv
            u_right = spread(right[tq], rq) * inv
            heads = {m: spread(cols[m][tq], rq) * inv for m in range(q + 1, SLAB)}
            for t in range(tq, SLAB // 8):
                coef = cols[q][t] * inv
                if t == tq:
                    coef = jnp.where(rows > rq, coef, 0.0)
                    scale = jnp.where(rows == rq, inv, 1.0)
                    left[t] = left[t] * scale
                    right[t] = right[t] * scale
                left[t] = left[t] - coef * u_left
                right[t] = right[t] - coef * u_right
                for m, head in heads.items():
                    cols[m][t] = cols[m][t] - coef * head
        for t in tiles:
            fac[lo + 8 * t : lo + 8 * t + 8, 0:128] = left[t]
            fac[lo + 8 * t : lo + 8 * t + 8, 128:256] = right[t]
        low = lo + SLAB
        if i % 2 == 1:
            between(i // 2)
        if low < 128:
            upper = jnp.concatenate(left, axis=0)
            wide = jnp.concatenate([upper, jnp.concatenate(right, axis=0)], axis=1)
            end = min(low + SLAB, 128)
            fac[low:end, :] = fac[low:end, :] - dot(upper[:, low:end], wide, 0, 0)
            if end < 128:
                fac[end:128, :] = fac[end:128, :] - dot(upper[:, end:128], wide, 0, 0)


def split(v):
    top = v.astype(jnp.bfloat16)
    return top, (v - top.astype(F32)).astype(jnp.bfloat16)


def dot3(p, q, ca, cb):
    def one(u, v):
        return lax.dot_general(u, v, (((ca,), (cb,)), ((), ())), preferred_element_type=F32)
    return one(p[0], q[0]) + (one(p[0], q[1]) + one(p[1], q[0]))


def factor(dd, pc, gl, wb, ub, fac, col, d_more, panel_wait, send):
    ident = (
        lax.broadcasted_iota(jnp.int32, (128, 128), 0)
        == lax.broadcasted_iota(jnp.int32, (128, 128), 1)
    ).astype(F32)

    def half(h, src, between, middle):
        lo, hi = slice(0, 128), slice(128, 256)
        fac[:, 0:128] = src[lo, lo]
        fac[:, 128:256] = ident
        factor_slabs(fac, lambda j: between(0, j))
        w0 = fac[:, 128:256]
        wb[h, lo, lo] = w0
        wb[h, lo, hi] = jnp.zeros((128, 128), F32)
        ub[h, lo, lo] = fac[:, 0:128]
        u01 = dot(w0, src[lo, hi])
        ub[h, lo, hi] = u01
        fac[:, 0:128] = src[hi, hi] - dot(u01, u01, 0, 0)
        fac[:, 128:256] = ident
        middle()
        factor_slabs(fac, lambda j: between(1, j))
        w1 = fac[:, 128:256]
        ub[h, hi, hi] = fac[:, 0:128]
        wb[h, hi, hi] = w1
        wb[h, hi, lo] = -dot(w1, dot(u01, w0, 0, 0))

    half(0, dd.at[0], d_more, lambda: None)
    w_one = wb[0]
    v = dot(w_one, dd[1])
    ub[1] = dd[2] - dot(v, v, 0, 0)
    w_one = split(w_one)
    v = split(v)
    kept = {}

    def middle():
        panel_wait()
        one = dot3(w_one, split(pc[0]), 1, 1)
        kept["one"] = dot3(w_one, split(one), 0, 0)
        kept["two"] = pc[1].T - dot3(v, split(one), 0, 0)
        kept["mix"] = split(dot3(w_one, v, 0, 0))

    half(1, ub.at[1], lambda b, j: None, middle)
    w_two = split(wb[1])
    two = dot3(w_two, split(kept["two"]), 1, 0)
    g_two = dot3(w_two, split(two), 0, 0)
    gl[256:512, :] = g_two

    @pl.when(col == 0)
    def _():
        gl[256:512, 0:256] = jnp.zeros((NB, NB), F32)

    @pl.when(col == 1)
    def _():
        gl[256:512, 0:256] = -wb[1].T
    send(1)
    gl[0:256, :] = kept["one"] - dot3(kept["mix"], split(g_two), 1, 0)

    @pl.when(col == 0)
    def _():
        gl[0:256, 0:256] = -wb[0].T

    @pl.when(col == 1)
    def _():
        gl[0:256, 0:256] = dot3(kept["mix"], w_two, 1, 1)
    send(0)
    tri = lax.broadcasted_iota(jnp.int32, (NB, NB), 0) >= lax.broadcasted_iota(jnp.int32, (NB, NB), 1)

    @pl.when(col < 2)
    def _():
        for h in range(2):
            gl[512:768, 256 * h : 256 * h + 256] = jnp.where(tri, ub[h].T, 0.0)
        send(2)


def update_kernel(a, rr, gl, out, hi, lo):
    row = lax.axis_index("row")
    col = lax.axis_index("col")
    slot = pl.program_id(0)

    @pl.when(slot == 0)
    def _():
        g = gl[0:512, :]
        top = g.astype(jnp.bfloat16)
        hi[...] = top
        lo[...] = (g - top.astype(F32)).astype(jnp.bfloat16)

    def mul(p, q):
        return jnp.dot(p, q, preferred_element_type=F32)

    acc = jnp.zeros((NB, 512), F32)
    for kk in range(2):
        r = rr[slot % 4, kk, pl.ds(pl.multiple_of(slot // 4 * NB, NB), NB), :]
        top = r.astype(jnp.bfloat16)
        rest = (r - top.astype(F32)).astype(jnp.bfloat16)
        rows = slice(kk * NB, kk * NB + NB)
        acc = acc + mul(top, hi[rows, :]) + (mul(top, lo[rows, :]) + mul(rest, hi[rows, :]))
    panel = (lax.broadcasted_iota(jnp.int32, (NB, 512), 1) < NB) & (col < 2)
    mine = a[pl.ds(pl.multiple_of(slot * NB, NB), NB), :]
    out[...] = jnp.where(panel, 0.0, mine) - acc

    @pl.when((slot == 0) & (row < 2))
    def _():
        out[:, 256:512] = jnp.zeros((NB, NB), F32)
        for q in range(2):
            @pl.when((row == q) & (col == q))
            def _():
                out[:, 0:256] = gl[512:768, 256 * q : 256 * q + 256]

        @pl.when((col > 1) | ((row == 0) & (col == 1)))
        def _():
            out[:, 0:256] = jnp.zeros((NB, NB), F32)


def update(kernel, rr, gl):
    vmem = pl.BlockSpec(memory_space=pltpu.VMEM)
    return pl.pallas_call(
        update_kernel,
        out_shape=jax.ShapeDtypeStruct(kernel.shape, F32),
        grid=(8,),
        in_specs=[vmem, vmem, vmem],
        out_specs=pl.BlockSpec((NB, 512), lambda j: (j, 0)),
        scratch_shapes=[pltpu.VMEM((512, 512), jnp.bfloat16)] * 2,
        compiler_params=pltpu.CompilerParams(vmem_limit_bytes=24 << 20),
        name="update_trailing",
    )(kernel, rr, gl)


def local(kernel):
    rr, gl, own = gather_and_factor(kernel)
    return update(own, rr, gl)


def solution(mesh):
    placed = (P("row", "col"),)
    return jax.shard_map(
        local, mesh=mesh, in_specs=placed, out_specs=P("row", "col"), check_vma=False
    )
```
